512 devices in a mesh: ctx: 64 (over z, y), tp: 8 (over x, core).
Axes of the slice: x: 4, y: 4, z: 16, core: 2. Of those that a mesh axis runs over, the one named last changes fastest.
Arguments:
- queries: bfloat16 [8192, 4096], P('ctx', 'tp'), may hold values from -6 to 6
- keys: bfloat16 [8192, 1024], P('ctx', 'tp'), may hold values from -6 to 6
- values: bfloat16 [8192, 1024], P('ctx', 'tp'), may hold values from -4 to 4
- w_out: bfloat16 [4096, 4096], P('tp'), may hold values from -0.09375 to 0.09375
- relevance_out: bfloat16 [8192, 4096], P('ctx', 'tp'), may hold values from -4 to 4
- segment_ids: int32 [8192], replicated, may hold values from 0 to 31, never falling along the last dimension, each value on 1 to 1024 neighbouring positions
Outputs:
- relevance_heads: bfloat16 [8192, 4096], P('ctx', 'tp')
- relevance_tokens: float32 [8192, 8], P('ctx', 'tp')
The draws below stay inside these ranges and needn't reach their ends.
Inputs may be any that keep to these rules, and one draw needn't show every extreme that they name: `segment_ids`: ids never fall along the prompt; every document holds 1 to 1024 tokens and one holds exactly 1024.
All inputs are finite; a program needn't handle non-finite values.
Results may differ from the reference program's by a relative error of at most 0.02.
Values may be sent and summed in bfloat16 or wider, within the bound.
A program may use at most 64 MiB of HBM per device.

```python
import math
import jax
import jax.numpy as jnp
import numpy as np
from jax import lax

KV_HEADS = 8
HEAD_DIM = 128
HEADS = 32
WIDTH = 4096
KBLK = 512
GROUP = 4
SEQ = 8192
MOST = 1024
DOCS = 32


def paired_fields(key):
    base = jax.random.fold_in(key, 2024)
    query_key, key_key = jax.random.split(base, 2)
    query_field = jnp.clip(jax.random.normal(query_key, (SEQ, KV_HEADS, GROUP, HEAD_DIM)), -6.0, 6.0)
    key_field = jnp.clip(jax.random.normal(key_key, (SEQ, KV_HEADS, HEAD_DIM)), -6.0, 6.0)
    return (query_field.reshape(SEQ, HEADS * HEAD_DIM), key_field.reshape(SEQ, KV_HEADS * HEAD_DIM))


def draw_queries(key, part):
    return paired_fields(key)[0].astype(jnp.bfloat16)


def draw_keys(key, part):
    return paired_fields(key)[1].astype(jnp.bfloat16)


def steps_of(key, shape, cuts, smallest, top_value):
    def one(axis_at, parts):
        heights = jax.random.uniform(jax.random.fold_in(jax.random.fold_in(key, 6), axis_at), (parts,), jnp.float32, smallest / len(cuts), top_value / len(cuts))
        return jnp.repeat(jnp.exp(heights), shape[axis_at] // parts).reshape((-1,) + (1,) * (len(shape) - axis_at - 1))

    gain = one(*cuts[0])
    for cut in cuts[1:]:
        gain = gain * one(*cut)
    return gain


def split_up(amount, total, limit, lean):
    weights = [(1 << 20) // math.isqrt(standing ** lean) + 1 for standing in range(2, amount + 1)]
    surplus, given = total - limit - (amount - 1), [1] * (amount - 1)
    while surplus > 0:
        movable = [i for i in range(amount - 1) if given[i] < limit]
        mass, budget = sum([weights[i] for i in movable]), surplus
        for i in movable:
            more = min(limit - given[i], max(1, budget * weights[i] // mass), surplus)
            given[i] = given[i] + more
            surplus = surplus - more
    return np.array([limit] + given)


def uneven(key, count, total, most, lean):
    if count == 2:
        one = jax.random.randint(key, (), max(1, total - most), min(most, total - 1) + 1)
        return jnp.stack([one, total - one])
    tallies = jnp.asarray(split_up(count, total, most, lean), jnp.int32)
    twos = (count - 1) // 2
    giver, receiver = tallies[1:1 + 2 * twos:2], tallies[2:2 + 2 * twos:2]
    room = jnp.minimum(giver - 1, most - receiver)
    shifted = jax.random.randint(jax.random.fold_in(key, 1), (twos,), 0, 1 << 20) % (room + 1)
    tallies = tallies.at[1:1 + 2 * twos:2].set(giver - shifted).at[2:2 + 2 * twos:2].set(receiver + shifted)
    return tallies[jax.random.permutation(jax.random.fold_in(key, 2), count)]


def scatter_about(stream_key, extent, width, reach, cuts=(), kind=jnp.bfloat16):
    values = width * jax.random.normal(stream_key, extent, jnp.float32)
    if cuts:
        values = values * steps_of(stream_key, extent, cuts, -0.22, 0.18)
    return jnp.clip(values, -reach, reach).astype(kind)


def setup_inputs(seed: int = 0) -> dict:
    streams_of = jax.random.split(jax.random.key(seed), 7)
    queries = draw_queries(jax.random.fold_in(streams_of[6], 71), 0)
    keys = draw_keys(jax.random.fold_in(streams_of[6], 71), 0)
    values = scatter_about(streams_of[2], (SEQ, KV_HEADS * HEAD_DIM), 1.0, 4.0, ((0, 64), (1, 8)))
    w_out = scatter_about(streams_of[3], (HEADS * HEAD_DIM, WIDTH), (HEADS * HEAD_DIM) ** -0.5, 0.09375, ((0, 8),))
    relevance_out = scatter_about(streams_of[4], (SEQ, WIDTH), 1.0, 4.0, ((0, 64), (1, 8)))
    segment_ids = jnp.searchsorted(jnp.cumsum(uneven(streams_of[5], DOCS, SEQ, MOST, 2)), jnp.arange(SEQ), side="right").astype(jnp.int32)
    return dict(queries=queries, keys=keys, values=values, w_out=w_out, relevance_out=relevance_out, segment_ids=segment_ids)


def block_mask(segment_ids, query_start, key_start, span):
    row_position = query_start + jnp.arange(KBLK, dtype=jnp.int32)
    key_position = key_start + jnp.arange(span, dtype=jnp.int32)
    row_segment = lax.dynamic_slice_in_dim(segment_ids, query_start, KBLK)
    key_segment = lax.dynamic_slice_in_dim(segment_ids, key_start, span)
    same = row_segment[:, None] == key_segment[None, :]
    return (same & (key_position[None, :] <= row_position[:, None]))[:, None, :]


def head_scores(query_head, key_head, segment_ids, block):
    span = MOST + KBLK
    query_start = (block * KBLK).astype(jnp.int32)
    key_start = jnp.clip(query_start - MOST, 0, SEQ - span).astype(jnp.int32)
    query_block = lax.dynamic_slice_in_dim(query_head, query_start, KBLK, 0).astype(jnp.float32)
    key_block = lax.dynamic_slice_in_dim(key_head, key_start, span, 0).astype(jnp.float32)
    scores = jnp.einsum('tgd,jd->tgj', query_block, key_block) * (HEAD_DIM ** -0.5)
    return scores, block_mask(segment_ids, query_start, key_start, span), key_start


def forward_head(query_head, key_head, value_head, segment_ids):
    span = MOST + KBLK

    def one_block(block):
        scores, visible, key_start = head_scores(query_head, key_head, segment_ids, block)
        row_max = jnp.max(jnp.where(visible, scores, -jnp.inf), axis=2)
        expo = jnp.where(visible, jnp.exp(scores - row_max[..., None]), 0.0)
        total = jnp.sum(expo, axis=2)
        weights = lax.optimization_barrier(expo.astype(jnp.bfloat16)).astype(jnp.float32)
        value_block = lax.dynamic_slice_in_dim(value_head, key_start, span, 0).astype(jnp.float32)
        summed = jnp.einsum('tgj,jd->tgd', weights, value_block)
        return (summed / total[..., None]).astype(jnp.bfloat16), row_max, total

    return lax.map(one_block, jnp.arange(SEQ // KBLK, dtype=jnp.int32))


def reference(queries, keys, values, w_out, relevance_out, segment_ids):
    query_heads = queries.reshape(SEQ, KV_HEADS, GROUP, HEAD_DIM).transpose(1, 0, 2, 3)
    key_heads = keys.reshape(SEQ, KV_HEADS, HEAD_DIM).transpose(1, 0, 2)
    value_heads = values.reshape(SEQ, KV_HEADS, HEAD_DIM).transpose(1, 0, 2)

    def forward_one(operands):
        return forward_head(operands[0], operands[1], operands[2], segment_ids)

    attended, row_max, total = lax.map(forward_one, (query_heads, key_heads, value_heads))
    attention = attended.reshape(KV_HEADS, SEQ, GROUP, HEAD_DIM).transpose(1, 0, 2, 3).reshape(SEQ, HEADS * HEAD_DIM)
    attention = lax.optimization_barrier(attention)
    projected = jnp.dot(attention, w_out, preferred_element_type=jnp.float32)
    upper = relevance_out.astype(jnp.float32)
    ratio = (upper * projected / (projected * projected + 1.0)).astype(jnp.bfloat16)
    carried_back = lax.dot_general(ratio, w_out, (((1,), (1,)), ((), ())), preferred_element_type=jnp.float32)
    attention_float = attention.astype(jnp.float32)
    carried = attention_float * carried_back
    relevance_heads = carried.astype(jnp.bfloat16)
    passed = (carried * attention_float / (attention_float * attention_float + 1.0)).astype(jnp.bfloat16)
    passed = lax.optimization_barrier(passed)
    passed_heads = passed.reshape(SEQ, KV_HEADS, GROUP, HEAD_DIM).transpose(1, 0, 2, 3)

    def backward_one(operands):
        query_head, key_head, value_head, passed_head, head_max, head_total = operands

        def accumulate(terms, inputs):
            block, block_max, block_total = inputs
            scores, visible, key_start = head_scores(query_head, key_head, segment_ids, block)
            share = jnp.where(visible, jnp.exp(scores - block_max[..., None]), 0.0) / block_total[..., None]
            passed_block = lax.dynamic_slice_in_dim(passed_head, (block * KBLK).astype(jnp.int32), KBLK, 0).astype(jnp.float32)
            value_block = lax.dynamic_slice_in_dim(value_head, key_start, MOST + KBLK, 0).astype(jnp.float32)
            inner = jnp.einsum('tgd,jd->tgj', passed_block, value_block)
            added = jnp.sum(share * inner, axis=(0, 1))
            current = lax.dynamic_slice_in_dim(terms, key_start, MOST + KBLK)
            return lax.dynamic_update_slice_in_dim(terms, current + added, key_start, 0), None

        blocks = jnp.arange(SEQ // KBLK, dtype=jnp.int32)
        terms, unused = lax.scan(accumulate, jnp.zeros((SEQ,), jnp.float32), (blocks, head_max, head_total))
        return terms

    token_terms = lax.map(backward_one, (query_heads, key_heads, value_heads, passed_heads, row_max, total))
    return relevance_heads, token_terms.T
```

```python
import jax
import jax.numpy as jnp
from jax import lax
from jax.experimental import pallas as pl
from jax.experimental.pallas import tpu as pltpu
from jax.sharding import PartitionSpec as P

MESH = pl.DeviceIdType.MESH
HEAD_DIM = 128
GROUP = 4
TOKENS = 128
ROWS = TOKENS * GROUP
SLOTS = 9
CTX = 64
XS = 4
FEAT = 512
HALF = TOKENS // 2
BF = jnp.bfloat16
F32 = jnp.float32
MASKED = -1e30
SCALE2 = HEAD_DIM ** (-0.5) * 1.4426950408889634


def dot_nt(a, b):
    return lax.dot_general(a, b, (((1,), (1,)), ((), ())), preferred_element_type=F32)


def dot_nn(a, b):
    return jnp.dot(a, b, preferred_element_type=F32)


def kernel(
    q_hbm, k_hbm, v_hbm, w_hbm, rel_hbm, seg_hbm, heads_hbm, tokens_ref,
    q, kv, w, rel, seg, score, weight, peak, att, send_two, from_far_left, from_far_right,
    merged_right, merged_left, direct_right, direct_left, in_left, in_right,
    ratio, cross_out, cross_in, heads, passed, inverse, term_out, term_in,
    local_sem, w_local_sem, w_send, w_recv, kv_send, kv_recv, a_send, a_recv,
    rs_send, rs_recv, ag_send, ag_recv, c_send, c_recv, t_send, t_recv,
):
    me = lax.axis_index("ctx")
    tp = lax.axis_index("tp")
    y = lax.rem(me, 4)
    core = lax.rem(tp, 2)
    x = lax.div(tp, 2)
    base = me - y
    y_right = base + lax.rem(y + 1, 4)
    y_left = base + lax.rem(y + 3, 4)
    up = lax.rem(me + 4, CTX)
    other = 1 - core
    partner = x * 2 + other
    x_right_i = lax.rem(x + 1, XS)
    x_left_i = lax.rem(x + 3, XS)
    x_far_i = lax.rem(x + 2, XS)
    x_right = x_right_i * 2 + core
    x_left = x_left_i * 2 + core

    def remote(src, dst, send, recv, ctx, tpi):
        return pltpu.make_async_remote_copy(
            src_ref=src, dst_ref=dst, send_sem=send, recv_sem=recv,
            device_id=(ctx, tpi), device_id_type=MESH,
        )

    loads = [
        pltpu.make_async_copy(k_hbm, kv.at[0, 0], local_sem.at[0]),
        pltpu.make_async_copy(v_hbm, kv.at[0, 1], local_sem.at[1]),
        pltpu.make_async_copy(seg_hbm, seg, local_sem.at[2]),
    ]
    for h in range(GROUP):
        loads.append(
            pltpu.make_async_copy(
                q_hbm.at[:, h * HEAD_DIM:(h + 1) * HEAD_DIM],
                q.at[h * TOKENS:(h + 1) * TOKENS, :],
                local_sem.at[3 + h],
            )
        )
    loads.append(pltpu.make_async_copy(rel_hbm, rel, local_sem.at[7]))
    for load in loads:
        load.start()

    barrier = pltpu.get_barrier_semaphore()

    def greet(ctx, tpi):
        pl.semaphore_signal(barrier, inc=1, device_id=(ctx, tpi), device_id_type=MESH)

    greet(me, partner)
    greet(me, x_right)
    greet(me, x_left)
    for d in range(1, SLOTS):
        greet(lax.rem(me + d, CTX), tp)
        greet(lax.rem(me + CTX - d, CTX), tp)
    pl.semaphore_wait(barrier, 19)

    def kv_copy(number, half, src, dst, ctx):
        return remote(
            kv.at[src, half], kv.at[dst, half], kv_send.at[number, half], kv_recv.at[dst, half], ctx, tp
        )

    def arrive(slot, half):
        remote(
            kv.at[slot, half], kv.at[slot, half], kv_send.at[0, half], kv_recv.at[slot, half], me, tp
        ).wait_recv()

    right_src = jnp.where(y < 3, 0, 8)
    right_dst = jnp.where(y < 3, 1, 5)
    left_src = jnp.where(y > 0, 8, 0)
    left_dst = jnp.where(y > 0, 7, 3)
    next_right_dst = jnp.where(y < 3, 5, 1)
    next_left_dst = jnp.where(y > 0, 3, 7)
    relay_right_src = jnp.where(y < 3, 1, 5)
    relay_left_src = jnp.where(y > 0, 7, 3)

    def up_one(half):
        return kv_copy(0, half, 0, 4, up)

    def up_two(half):
        return kv_copy(1, half, 4, 8, up)

    def right_zero(half):
        return kv_copy(2, half, right_src, right_dst, y_right)

    def left_zero(half):
        return kv_copy(3, half, left_src, left_dst, y_left)

    def right_one(half):
        return kv_copy(4, half, 4, next_right_dst, y_right)

    def left_one(half):
        return kv_copy(5, half, 4, next_left_dst, y_left)

    def relay_right(half):
        return kv_copy(6, half, relay_right_src, 2, y_right)

    def relay_left(half):
        return kv_copy(7, half, relay_left_src, 6, y_left)

    loads[0].wait()
    up_one(0).start()
    loads[1].wait()
    up_one(1).start()

    @pl.when(y < 3)
    def _():
        right_zero(0).start()
        right_zero(1).start()

    @pl.when(y == 0)
    def _():
        left_zero(0).start()
        left_zero(1).start()

    w_copies = []
    for i in range(XS):
        w_copies.append(
            pltpu.make_async_copy(
                w_hbm.at[:, pl.ds(pl.multiple_of((2 * i + core) * FEAT, FEAT), FEAT)],
                w.at[core, i], w_local_sem.at[i],
            )
        )
        w_copies.append(
            remote(
                w_hbm.at[:, pl.ds(pl.multiple_of((2 * i + other) * FEAT, FEAT), FEAT)],
                w.at[core, i], w_send.at[i], w_recv.at[i], me, partner,
            )
        )
    for copy in w_copies:
        copy.start()

    for load in loads[2:]:
        load.wait()

    own_seg = jnp.broadcast_to(seg[pl.ds(me, 1), :].astype(F32), (TOKENS, TOKENS)).T
    row_at = lax.broadcasted_iota(jnp.int32, (TOKENS, TOKENS), 0)
    key_at = lax.broadcasted_iota(jnp.int32, (TOKENS, TOKENS), 1)

    def score_block(slot, first=False):
        key_seg = seg[pl.ds(lax.rem(me + CTX - slot, CTX), 1), :].astype(F32)
        visible = own_seg == key_seg
        if first:
            visible = visible & (key_at <= row_at)
        for h in range(GROUP):
            rows = pl.ds(h * TOKENS, TOKENS)
            s = dot_nt(q[rows, :], kv[slot, 0])
            s = jnp.where(visible, s, MASKED)
            score[slot, rows, :] = s
            if first:
                peak[rows, :] = s
            else:
                peak[rows, :] = jnp.maximum(peak[rows, :], s)

    score_block(0, True)

    for half in range(2):
        arrive(4, half)
        up_two(half).start()
        right_one(half).start()
        left_one(half).start()
    score_block(4)

    inner_y = (y == 1) | (y == 2)
    outer_y = (y == 0) | (y == 3)

    @pl.when(y > 0)
    def _():
        for half in range(2):
            arrive(1, half)

            @pl.when(y < 3)
            def _():
                relay_right(half).start()

    @pl.when(y == 3)
    def _():
        for half in range(2):
            arrive(3, half)

    for half in range(2):
        arrive(8, half)

        @pl.when(y > 0)
        def _():
            left_zero(half).start()

        @pl.when(y == 3)
        def _():
            right_zero(half).start()

    score_block(jnp.where(y > 0, 1, 8))

    one_left = jnp.where(y > 0, 5, 1)
    one_right = jnp.where(y < 3, 3, 7)
    for half in range(2):
        arrive(one_left, half)

        @pl.when(outer_y)
        def _():
            relay_right(half).start()

        arrive(one_right, half)

        @pl.when(outer_y)
        def _():
            relay_left(half).start()

    score_block(jnp.where(y > 0, 8, 1))
    score_block(5 - jnp.where(y > 0, 0, 2))
    @pl.when(y == 0)
    def _():
        for half in range(2):
            arrive(5, half)

    @pl.when(y < 3)
    def _():
        for half in range(2):
            arrive(7, half)

            @pl.when(inner_y)
            def _():
                relay_left(half).start()

    score_block(jnp.where(y > 0, 3, 5))
    score_block(7)
    for half in range(2):
        arrive(2, half)
    score_block(2)
    for half in range(2):
        arrive(6, half)
    score_block(6)

    values = kv[:, 1].reshape(SLOTS * TOKENS, HEAD_DIM)
    for h in range(GROUP):
        rows = pl.ds(h * TOKENS, TOKENS)
        top = jnp.max(peak[rows, :], axis=1, keepdims=True)
        top = jnp.broadcast_to(top, (TOKENS, TOKENS))
        total = jnp.zeros((TOKENS, TOKENS), F32)
        for slot in range(SLOTS):
            e = jnp.exp2((score[slot, rows, :] - top) * SCALE2)
            total = total + e
            score[slot, rows, :] = e
            weight[rows, slot * TOKENS:(slot + 1) * TOKENS] = e.astype(BF)
        inv = 1.0 / jnp.broadcast_to(jnp.sum(total, axis=1, keepdims=True), (TOKENS, TOKENS))
        columns = slice(h * HEAD_DIM, (h + 1) * HEAD_DIM)
        inverse[:, columns] = inv
        summed = dot_nn(weight[rows, :], values)
        att[core, :, columns] = (summed * inv).astype(BF)

    a_copy = remote(att.at[core], att.at[core], a_send, a_recv, me, partner)
    a_copy.start()
    for copy in w_copies[0::2]:
        copy.wait()
    for copy in w_copies[1::2]:
        copy.wait_recv()
    remote(att.at[other], att.at[other], a_send, a_recv, me, partner).wait_recv()

    def project(i):
        return dot_nn(att[core], w[core, i]) + dot_nn(att[other], w[other, i])

    def rs(number, src, dst, tpi):
        return remote(src, dst, rs_send.at[number], rs_recv.at[number], me, tpi)

    send_two[...] = project(x_far_i).astype(BF)
    top_rows, low_rows = pl.ds(0, HALF), pl.ds(HALF, HALF)
    far_right = rs(0, send_two.at[top_rows], from_far_left, x_right)
    far_left = rs(1, send_two.at[low_rows], from_far_right, x_left)
    far_right.start()
    far_left.start()
    to_right = project(x_right_i)
    direct_right[...] = to_right[HALF:].astype(BF)
    near_right = rs(2, direct_right, in_left.at[low_rows], x_right)
    near_right.start()
    to_left = project(x_left_i)
    direct_left[...] = to_left[:HALF].astype(BF)
    near_left = rs(3, direct_left, in_right.at[top_rows], x_left)
    near_left.start()
    far_right.wait_recv()
    merged_right[...] = (to_right[:HALF] + from_far_left[...].astype(F32)).astype(BF)
    last_right = rs(4, merged_right, in_left.at[top_rows], x_right)
    last_right.start()
    far_left.wait_recv()
    merged_left[...] = (to_left[HALF:] + from_far_right[...].astype(F32)).astype(BF)
    last_left = rs(5, merged_left, in_right.at[low_rows], x_left)
    last_left.start()
    mine = project(x)
    for copy in (near_right, near_left, last_right, last_left):
        copy.wait_recv()

    total = mine + in_left[...].astype(F32) + in_right[...].astype(F32)
    ratio[x] = (rel[...].astype(F32) * total / (total * total + 1.0)).astype(BF)

    def ag(number, owner, rows, tpi):
        return remote(
            ratio.at[owner, rows], ratio.at[owner, rows], ag_send.at[number], ag_recv.at[number], me, tpi
        )

    shares = [
        ag(0, x, top_rows, x_right), ag(1, x, low_rows, x_left),
        ag(2, x, low_rows, x_right), ag(3, x, top_rows, x_left),
    ]
    for copy in shares:
        copy.start()
    back_other = dot_nt(ratio[x], w[other, x])
    back_own = dot_nt(ratio[x], w[core, x])
    ag(0, x_left_i, top_rows, x_right).wait_recv()
    pass_right = ag(4, x_left_i, top_rows, x_right)
    pass_right.start()
    ag(1, x_right_i, low_rows, x_left).wait_recv()
    pass_left = ag(5, x_right_i, low_rows, x_left)
    pass_left.start()
    ag(2, x_left_i, low_rows, x_right).wait_recv()
    back_other += dot_nt(ratio[x_left_i], w[other, x_left_i])
    back_own += dot_nt(ratio[x_left_i], w[core, x_left_i])
    ag(3, x_right_i, top_rows, x_left).wait_recv()
    back_other += dot_nt(ratio[x_right_i], w[other, x_right_i])
    back_own += dot_nt(ratio[x_right_i], w[core, x_right_i])
    ag(4, x_far_i, top_rows, x_right).wait_recv()
    ag(5, x_far_i, low_rows, x_left).wait_recv()
    back_other += dot_nt(ratio[x_far_i], w[other, x_far_i])
    cross_out[...] = back_other.astype(BF)
    cross = remote(cross_out, cross_in, c_send, c_recv, me, partner)
    cross.start()
    back_own += dot_nt(ratio[x_far_i], w[core, x_far_i])
    cross.wait_recv()
    a = att[core].astype(F32)
    carried = a * (back_own + cross_in[...].astype(F32))
    heads[...] = carried.astype(BF)
    heads_copy = pltpu.make_async_copy(heads, heads_hbm, local_sem.at[0])
    heads_copy.start()
    scaled = carried * a / (a * a + 1.0) * inverse[...]
    for h in range(GROUP):
        passed[h * TOKENS:(h + 1) * TOKENS, :] = scaled[:, h * HEAD_DIM:(h + 1) * HEAD_DIM].astype(BF)

    def term(slot):
        inner = dot_nt(passed[...], kv[slot, 1])
        return jnp.sum(score[slot] * inner, axis=0, keepdims=True)

    def term_copy(slot):
        return remote(
            term_out.at[slot], term_in.at[slot], t_send.at[slot], t_recv.at[slot],
            lax.rem(me + CTX - slot, CTX), tp,
        )

    for slot in range(SLOTS - 1, 0, -1):
        term_out[slot] = term(slot)
        term_copy(slot).start()
    own = term(0)
    for slot in range(1, SLOTS):
        term_copy(slot).wait_recv()
        own = own + term_in[slot]
    tokens_ref[...] = jnp.broadcast_to(own, (TOKENS, TOKENS)).T[:, 0:1]

    heads_copy.wait()
    for copy in w_copies[1::2]:
        copy.wait_send()
    for half in range(2):
        for make in (up_one, up_two, right_zero, left_zero, right_one, left_one, relay_right, relay_left):
            make(half).wait_send()
    a_copy.wait_send()
    for copy in (far_right, far_left, near_right, near_left, last_right, last_left):
        copy.wait_send()
    for copy in shares + [pass_right, pass_left]:
        copy.wait_send()
    cross.wait_send()
    for slot in range(1, SLOTS):
        term_copy(slot).wait_send()


def on_device(queries, keys, values, w_out, relevance_out, segment_ids):
    anywhere = pl.BlockSpec(memory_space=pl.ANY)
    vmem, dma = pltpu.VMEM, pltpu.SemaphoreType.DMA
    return pl.pallas_call(
        kernel,
        out_shape=(
            jax.ShapeDtypeStruct((TOKENS, GROUP * HEAD_DIM), BF),
            jax.ShapeDtypeStruct((TOKENS, 1), F32),
        ),
        in_specs=[anywhere] * 6,
        out_specs=(anywhere, pl.BlockSpec(memory_space=pltpu.VMEM)),
        scratch_shapes=[
            vmem((ROWS, HEAD_DIM), BF),
            vmem((SLOTS, 2, TOKENS, HEAD_DIM), BF),
            vmem((2, XS, FEAT, FEAT), BF),
            vmem((TOKENS, FEAT), BF),
            vmem((CTX, TOKENS), jnp.int32),
            vmem((SLOTS, ROWS, TOKENS), F32),
            vmem((ROWS, SLOTS * TOKENS), BF),
            vmem((ROWS, TOKENS), F32),
            vmem((2, TOKENS, FEAT), BF),
            vmem((TOKENS, FEAT), BF),
            vmem((HALF, FEAT), BF),
            vmem((HALF, FEAT), BF),
            vmem((HALF, FEAT), BF),
            vmem((HALF, FEAT), BF),
            vmem((HALF, FEAT), BF),
            vmem((HALF, FEAT), BF),
            vmem((TOKENS, FEAT), BF),
            vmem((TOKENS, FEAT), BF),
            vmem((XS, TOKENS, FEAT), BF),
            vmem((TOKENS, FEAT), BF),
            vmem((TOKENS, FEAT), BF),
            vmem((TOKENS, FEAT), BF),
            vmem((ROWS, HEAD_DIM), BF),
            vmem((TOKENS, FEAT), F32),
            vmem((SLOTS, 1, TOKENS), F32),
            vmem((SLOTS, 1, TOKENS), F32),
            dma((8,)), dma((XS,)), dma((XS,)), dma((XS,)),
            dma((8, 2)), dma((SLOTS, 2)), dma, dma,
            dma((6,)), dma((6,)), dma((6,)), dma((6,)), dma, dma,
            dma((SLOTS,)), dma((SLOTS,)),
        ],
        compiler_params=pltpu.CompilerParams(
            collective_id=0, has_side_effects=True, vmem_limit_bytes=60 << 20
        ),
        name="relevance",
    )(queries, keys, values, w_out, relevance_out, segment_ids.reshape(CTX, TOKENS))


def solution(mesh):
    placed = (P("ctx", "tp"), P("ctx", "tp"), P("ctx", "tp"), P("tp", None), P("ctx", "tp"), P())
    return jax.shard_map(
        on_device,
        mesh=mesh,
        in_specs=placed,
        out_specs=(P("ctx", "tp"), P("ctx", "tp")),
        check_vma=False,
    )
```

```python
import jax
import jax.numpy as jnp
from jax import lax
from jax.experimental import pallas as pl
from jax.experimental.pallas import tpu as pltpu
from jax.sharding import PartitionSpec as P

MESH = pl.DeviceIdType.MESH
HEAD_DIM = 128
GROUP = 4
TOKENS = 128
ROWS = TOKENS * GROUP
SLOTS = 9
CTX = 64
XS = 4
FEAT = 512
HALF = TOKENS // 2
BF = jnp.bfloat16
F32 = jnp.float32
MASKED = -1e30
SCALE2 = HEAD_DIM ** (-0.5) * 1.4426950408889634


def dot_nt(a, b):
    return lax.dot_general(a, b, (((1,), (1,)), ((), ())), preferred_element_type=F32)


def dot_nn(a, b):
    return jnp.dot(a, b, preferred_element_type=F32)


def kernel(
    q_hbm, k_hbm, v_hbm, w_hbm, rel_hbm, seg_hbm, heads_hbm, tokens_ref,
    q, kv, w, rel, seg, score, weight, peak, att, send_two, from_far_left, from_far_right,
    merged_right, merged_left, direct_right, direct_left, in_left, in_right,
    ratio, cross_out, cross_in, heads, passed, inverse, term_out, term_in,
    local_sem, w_local_sem, w_send, w_recv, kv_send, kv_recv, a_send, a_recv,
    rs_send, rs_recv, ag_send, ag_recv, c_send, c_recv, t_send, t_recv,
):
    me = lax.axis_index("ctx")
    tp = lax.axis_index("tp")
    y = lax.rem(me, 4)
    core = lax.rem(tp, 2)
    x = lax.div(tp, 2)
    base = me - y
    y_right = base + lax.rem(y + 1, 4)
    y_left = base + lax.rem(y + 3, 4)
    up = me + 4
    other = 1 - core
    partner = x * 2 + other
    x_right_i = lax.rem(x + 1, XS)
    x_left_i = lax.rem(x + 3, XS)
    x_far_i = lax.rem(x + 2, XS)
    x_right = x_right_i * 2 + core
    x_left = x_left_i * 2 + core

    def remote(src, dst, send, recv, ctx, tpi):
        return pltpu.make_async_remote_copy(
            src_ref=src, dst_ref=dst, send_sem=send, recv_sem=recv,
            device_id=(ctx, tpi), device_id_type=MESH,
        )

    loads = [
        pltpu.make_async_copy(k_hbm, kv.at[0, 0], local_sem.at[0]),
        pltpu.make_async_copy(v_hbm, kv.at[0, 1], local_sem.at[1]),
        pltpu.make_async_copy(seg_hbm, seg, local_sem.at[2]),
    ]
    for h in range(GROUP):
        loads.append(
            pltpu.make_async_copy(
                q_hbm.at[:, h * HEAD_DIM:(h + 1) * HEAD_DIM],
                q.at[h * TOKENS:(h + 1) * TOKENS, :],
                local_sem.at[3 + h],
            )
        )
    loads.append(pltpu.make_async_copy(rel_hbm, rel, local_sem.at[7]))
    for load in loads:
        load.start()

    barrier = pltpu.get_barrier_semaphore()

    def greet(ctx, tpi):
        pl.semaphore_signal(barrier, inc=1, device_id=(ctx, tpi), device_id_type=MESH)

    greet(me, partner)
    greet(me, x_right)
    greet(me, x_left)
    greet(y_right, tp)
    greet(y_left, tp)

    @pl.when(me < CTX - 4)
    def _():
        greet(me + 4, tp)

    @pl.when(me >= 4)
    def _():
        greet(me - 4, tp)

    @pl.when(me < SLOTS - 1)
    def _():
        for d in range(1, SLOTS):
            @pl.when(me < d)
            def _():
                kv[d] = jnp.zeros((2, TOKENS, HEAD_DIM), BF)

    pl.semaphore_wait(
        barrier, 5 + jnp.where(me < CTX - 4, 1, 0) + jnp.where(me >= 4, 1, 0)
    )

    def kv_copy(number, half, src, dst, ctx):
        return (
            remote(
                kv.at[src, half], kv.at[dst, half], kv_send.at[number, half], kv_recv.at[dst, half], ctx, tp
            ),
            (ctx >= dst) & (ctx < CTX),
        )

    def start(pair):
        copy, exists = pair

        @pl.when(exists)
        def _():
            copy.start()

    def arrive(slot, half):
        @pl.when(me >= slot)
        def _():
            remote(
                kv.at[slot, half], kv.at[slot, half], kv_send.at[0, half], kv_recv.at[slot, half], me, tp
            ).wait_recv()

    right_src = jnp.where(y < 3, 0, 8)
    right_dst = jnp.where(y < 3, 1, 5)
    left_src = jnp.where(y > 0, 8, 0)
    left_dst = jnp.where(y > 0, 7, 3)
    next_right_dst = jnp.where(y < 3, 5, 1)
    next_left_dst = jnp.where(y > 0, 3, 7)
    relay_right_src = jnp.where(y < 3, 1, 5)
    relay_left_src = jnp.where(y > 0, 7, 3)

    def up_one(half):
        return kv_copy(0, half, 0, 4, up)

    def up_two(half):
        return kv_copy(1, half, 4, 8, up)

    def right_zero(half):
        return kv_copy(2, half, right_src, right_dst, y_right)

    def left_zero(half):
        return kv_copy(3, half, left_src, left_dst, y_left)

    def right_one(half):
        return kv_copy(4, half, 4, next_right_dst, y_right)

    def left_one(half):
        return kv_copy(5, half, 4, next_left_dst, y_left)

    def relay_right(half):
        return kv_copy(6, half, relay_right_src, 2, y_right)

    def relay_left(half):
        return kv_copy(7, half, relay_left_src, 6, y_left)

    loads[0].wait()
    start(up_one(0))
    loads[1].wait()
    start(up_one(1))

    @pl.when(y < 3)
    def _():
        start(right_zero(0))
        start(right_zero(1))

    @pl.when(y == 0)
    def _():
        start(left_zero(0))
        start(left_zero(1))

    w_copies = []
    for i in range(XS):
        w_copies.append(
            pltpu.make_async_copy(
                w_hbm.at[:, pl.ds(pl.multiple_of((2 * i + core) * FEAT, FEAT), FEAT)],
                w.at[core, i], w_local_sem.at[i],
            )
        )
        w_copies.append(
            remote(
                w_hbm.at[:, pl.ds(pl.multiple_of((2 * i + other) * FEAT, FEAT), FEAT)],
                w.at[core, i], w_send.at[i], w_recv.at[i], me, partner,
            )
        )
    for copy in w_copies:
        copy.start()

    for load in loads[2:]:
        load.wait()

    own_seg = jnp.broadcast_to(seg[pl.ds(me, 1), :].astype(F32), (TOKENS, TOKENS)).T
    row_at = lax.broadcasted_iota(jnp.int32, (TOKENS, TOKENS), 0)
    key_at = lax.broadcasted_iota(jnp.int32, (TOKENS, TOKENS), 1)

    def score_block(slot, first=False):
        key_seg = seg[pl.ds(lax.rem(me + CTX - slot, CTX), 1), :].astype(F32)
        visible = own_seg == key_seg
        if first:
            visible = visible & (key_at <= row_at)
        for h in range(GROUP):
            rows = pl.ds(h * TOKENS, TOKENS)
            s = dot_nt(q[rows, :], kv[slot, 0])
            s = jnp.where(visible, s, MASKED)
            score[slot, rows, :] = s
            if first:
                peak[rows, :] = s
            else:
                peak[rows, :] = jnp.maximum(peak[rows, :], s)

    score_block(0, True)

    for half in range(2):
        arrive(4, half)
        start(up_two(half))
        start(right_one(half))
        start(left_one(half))
    score_block(4)

    inner_y = (y == 1) | (y == 2)
    outer_y = (y == 0) | (y == 3)

    @pl.when(y > 0)
    def _():
        for half in range(2):
            arrive(1, half)

            @pl.when(y < 3)
            def _():
                start(relay_right(half))

    @pl.when(y == 3)
    def _():
        for half in range(2):
            arrive(3, half)

    for half in range(2):
        arrive(8, half)

        @pl.when(y > 0)
        def _():
            start(left_zero(half))

        @pl.when(y == 3)
        def _():
            start(right_zero(half))

    score_block(jnp.where(y > 0, 1, 8))

    one_left = jnp.where(y > 0, 5, 1)
    one_right = jnp.where(y < 3, 3, 7)
    for half in range(2):
        arrive(one_left, half)

        @pl.when(outer_y)
        def _():
            start(relay_right(half))

        arrive(one_right, half)

        @pl.when(outer_y)
        def _():
            start(relay_left(half))

    score_block(jnp.where(y > 0, 8, 1))
    score_block(5 - jnp.where(y > 0, 0, 2))
    @pl.when(y == 0)
    def _():
        for half in range(2):
            arrive(5, half)

    @pl.when(y < 3)
    def _():
        for half in range(2):
            arrive(7, half)

            @pl.when(inner_y)
            def _():
                start(relay_left(half))

    score_block(jnp.where(y > 0, 3, 5))
    score_block(7)
    for half in range(2):
        arrive(2, half)
    score_block(2)
    for half in range(2):
        arrive(6, half)
    score_block(6)

    values = kv[:, 1].reshape(SLOTS * TOKENS, HEAD_DIM)
    for h in range(GROUP):
        rows = pl.ds(h * TOKENS, TOKENS)
        top = jnp.max(peak[rows, :], axis=1, keepdims=True)
        top = jnp.broadcast_to(top, (TOKENS, TOKENS))
        total = jnp.zeros((TOKENS, TOKENS), F32)
        for slot in range(SLOTS):
            e = jnp.exp2((score[slot, rows, :] - top) * SCALE2)
            total = total + e
            score[slot, rows, :] = e
            weight[rows, slot * TOKENS:(slot + 1) * TOKENS] = e.astype(BF)
        inv = 1.0 / jnp.broadcast_to(jnp.sum(total, axis=1, keepdims=True), (TOKENS, TOKENS))
        columns = slice(h * HEAD_DIM, (h + 1) * HEAD_DIM)
        inverse[:, columns] = inv
        summed = dot_nn(weight[rows, :], values)
        att[core, :, columns] = (summed * inv).astype(BF)

    a_copy = remote(att.at[core], att.at[core], a_send, a_recv, me, partner)
    a_copy.start()
    for copy in w_copies[0::2]:
        copy.wait()
    for copy in w_copies[1::2]:
        copy.wait_recv()
    remote(att.at[other], att.at[other], a_send, a_recv, me, partner).wait_recv()

    def project(i):
        return dot_nn(att[core], w[core, i]) + dot_nn(att[other], w[other, i])

    def rs(number, src, dst, tpi):
        return remote(src, dst, rs_send.at[number], rs_recv.at[number], me, tpi)

    send_two[...] = project(x_far_i).astype(BF)
    top_rows, low_rows = pl.ds(0, HALF), pl.ds(HALF, HALF)
    far_right = rs(0, send_two.at[top_rows], from_far_left, x_right)
    far_left = rs(1, send_two.at[low_rows], from_far_right, x_left)
    far_right.start()
    far_left.start()
    to_right = project(x_right_i)
    direct_right[...] = to_right[HALF:].astype(BF)
    near_right = rs(2, direct_right, in_left.at[low_rows], x_right)
    near_right.start()
    to_left = project(x_left_i)
    direct_left[...] = to_left[:HALF].astype(BF)
    near_left = rs(3, direct_left, in_right.at[top_rows], x_left)
    near_left.start()
    far_right.wait_recv()
    merged_right[...] = (to_right[:HALF] + from_far_left[...].astype(F32)).astype(BF)
    last_right = rs(4, merged_right, in_left.at[top_rows], x_right)
    last_right.start()
    far_left.wait_recv()
    merged_left[...] = (to_left[HALF:] + from_far_right[...].astype(F32)).astype(BF)
    last_left = rs(5, merged_left, in_right.at[low_rows], x_left)
    last_left.start()
    mine = project(x)
    for copy in (near_right, near_left, last_right, last_left):
        copy.wait_recv()

    total = mine + in_left[...].astype(F32) + in_right[...].astype(F32)
    ratio[x] = (rel[...].astype(F32) * total / (total * total + 1.0)).astype(BF)

    def ag(number, owner, rows, tpi):
        return remote(
            ratio.at[owner, rows], ratio.at[owner, rows], ag_send.at[number], ag_recv.at[number], me, tpi
        )

    shares = [
        ag(0, x, top_rows, x_right), ag(1, x, low_rows, x_left),
        ag(2, x, low_rows, x_right), ag(3, x, top_rows, x_left),
    ]
    for copy in shares:
        copy.start()
    back_other = dot_nt(ratio[x], w[other, x])
    back_own = dot_nt(ratio[x], w[core, x])
    ag(0, x_left_i, top_rows, x_right).wait_recv()
    pass_right = ag(4, x_left_i, top_rows, x_right)
    pass_right.start()
    ag(1, x_right_i, low_rows, x_left).wait_recv()
    pass_left = ag(5, x_right_i, low_rows, x_left)
    pass_left.start()
    ag(2, x_left_i, low_rows, x_right).wait_recv()
    back_other += dot_nt(ratio[x_left_i], w[other, x_left_i])
    back_own += dot_nt(ratio[x_left_i], w[core, x_left_i])
    ag(3, x_right_i, top_rows, x_left).wait_recv()
    back_other += dot_nt(ratio[x_right_i], w[other, x_right_i])
    back_own += dot_nt(ratio[x_right_i], w[core, x_right_i])
    ag(4, x_far_i, top_rows, x_right).wait_recv()
    ag(5, x_far_i, low_rows, x_left).wait_recv()
    back_other += dot_nt(ratio[x_far_i], w[other, x_far_i])
    cross_out[...] = back_other.astype(BF)
    cross = remote(cross_out, cross_in, c_send, c_recv, me, partner)
    cross.start()
    back_own += dot_nt(ratio[x_far_i], w[core, x_far_i])
    cross.wait_recv()
    a = att[core].astype(F32)
    carried = a * (back_own + cross_in[...].astype(F32))
    heads[...] = carried.astype(BF)
    heads_copy = pltpu.make_async_copy(heads, heads_hbm, local_sem.at[0])
    heads_copy.start()
    scaled = carried * a / (a * a + 1.0) * inverse[...]
    for h in range(GROUP):
        passed[h * TOKENS:(h + 1) * TOKENS, :] = scaled[:, h * HEAD_DIM:(h + 1) * HEAD_DIM].astype(BF)

    def term(slot):
        inner = dot_nt(passed[...], kv[slot, 1])
        return jnp.sum(score[slot] * inner, axis=0, keepdims=True)

    def term_copy(slot):
        return remote(
            term_out.at[slot], term_in.at[slot], t_send.at[slot], t_recv.at[slot],
            me - slot, tp,
        )

    for slot in range(SLOTS - 1, 0, -1):
        term_out[slot] = term(slot)

        @pl.when(me >= slot)
        def _():
            term_copy(slot).start()

        @pl.when(me + slot >= CTX)
        def _():
            term_in[slot] = jnp.zeros((1, TOKENS), F32)

    own = term(0)
    for slot in range(1, SLOTS):
        @pl.when(me + slot < CTX)
        def _():
            term_copy(slot).wait_recv()

        own = own + term_in[slot]
    tokens_ref[...] = own

    heads_copy.wait()
    for copy in w_copies[1::2]:
        copy.wait_send()
    for half in range(2):
        for make in (up_one, up_two, right_zero, left_zero, right_one, left_one, relay_right, relay_left):
            copy, exists = make(half)

            @pl.when(exists)
            def _():
                copy.wait_send()
    a_copy.wait_send()
    for copy in (far_right, far_left, near_right, near_left, last_right, last_left):
        copy.wait_send()
    for copy in shares + [pass_right, pass_left]:
        copy.wait_send()
    cross.wait_send()
    for slot in range(1, SLOTS):
        @pl.when(me >= slot)
        def _():
            term_copy(slot).wait_send()


def on_device(queries, keys, values, w_out, relevance_out, segment_ids):
    anywhere = pl.BlockSpec(memory_space=pl.ANY)
    vmem, dma = pltpu.VMEM, pltpu.SemaphoreType.DMA
    heads, tokens = pl.pallas_call(
        kernel,
        out_shape=(
            jax.ShapeDtypeStruct((TOKENS, GROUP * HEAD_DIM), BF),
            jax.ShapeDtypeStruct((1, TOKENS), F32),
        ),
        in_specs=[anywhere] * 6,
        out_specs=(anywhere, pl.BlockSpec(memory_space=pltpu.VMEM)),
        scratch_shapes=[
            vmem((ROWS, HEAD_DIM), BF),
            vmem((SLOTS, 2, TOKENS, HEAD_DIM), BF),
            vmem((2, XS, FEAT, FEAT), BF),
            vmem((TOKENS, FEAT), BF),
            vmem((CTX, TOKENS), jnp.int32),
            vmem((SLOTS, ROWS, TOKENS), F32),
            vmem((ROWS, SLOTS * TOKENS), BF),
            vmem((ROWS, TOKENS), F32),
            vmem((2, TOKENS, FEAT), BF),
            vmem((TOKENS, FEAT), BF),
            vmem((HALF, FEAT), BF),
            vmem((HALF, FEAT), BF),
            vmem((HALF, FEAT), BF),
            vmem((HALF, FEAT), BF),
            vmem((HALF, FEAT), BF),
            vmem((HALF, FEAT), BF),
            vmem((TOKENS, FEAT), BF),
            vmem((TOKENS, FEAT), BF),
            vmem((XS, TOKENS, FEAT), BF),
            vmem((TOKENS, FEAT), BF),
            vmem((TOKENS, FEAT), BF),
            vmem((TOKENS, FEAT), BF),
            vmem((ROWS, HEAD_DIM), BF),
            vmem((TOKENS, FEAT), F32),
            vmem((SLOTS, 1, TOKENS), F32),
            vmem((SLOTS, 1, TOKENS), F32),
            dma((8,)), dma((XS,)), dma((XS,)), dma((XS,)),
            dma((8, 2)), dma((SLOTS, 2)), dma, dma,
            dma((6,)), dma((6,)), dma((6,)), dma((6,)), dma, dma,
            dma((SLOTS,)), dma((SLOTS,)),
        ],
        compiler_params=pltpu.CompilerParams(
            collective_id=0, has_side_effects=True, vmem_limit_bytes=60 << 20
        ),
        name="relevance",
    )(queries, keys, values, w_out, relevance_out, segment_ids.reshape(CTX, TOKENS))
    return heads, tokens.T


def solution(mesh):
    placed = (P("ctx", "tp"), P("ctx", "tp"), P("ctx", "tp"), P("tp", None), P("ctx", "tp"), P())
    return jax.shard_map(
        on_device,
        mesh=mesh,
        in_specs=placed,
        out_specs=(P("ctx", "tp"), P("ctx", "tp")),
        check_vma=False,
    )
```

```python
import jax
import jax.numpy as jnp
from jax import lax
from jax.experimental import pallas as pl
from jax.experimental.pallas import tpu as pltpu
from jax.sharding import PartitionSpec as P

MESH = pl.DeviceIdType.MESH
HEAD_DIM = 128
GROUP = 4
TOKENS = 128
ROWS = TOKENS * GROUP
SLOTS = 9
CTX = 64
XS = 4
FEAT = 512
QUARTER = TOKENS // 4
BF = jnp.bfloat16
F32 = jnp.float32
MASKED = -1e30
SCALE2 = HEAD_DIM ** (-0.5) * 1.4426950408889634


def dot_nt(a, b):
    return lax.dot_general(a, b, (((1,), (1,)), ((), ())), preferred_element_type=F32)


def dot_nn(a, b):
    return jnp.dot(a, b, preferred_element_type=F32)


def kernel(
    q_hbm, k_hbm, v_hbm, w_hbm, rel_hbm, seg_hbm, heads, tokens_ref,
    q, kv, w, rel, seg, score, weight, peak, att, far_out, far_in, right_out, left_out, left_in, right_in, near,
    ratio, cross_out, cross_in, values_flipped, passed, inverse, term_out, term_in,
    local_sem, w_local_sem, w_send, w_recv, kv_send, kv_recv, a_send, a_recv,
    rs_send, rs_recv, ag_send, ag_recv, c_send, c_recv, t_send, t_recv,
):
    me = lax.axis_index("ctx")
    tp = lax.axis_index("tp")
    y = lax.rem(me, 4)
    core = lax.rem(tp, 2)
    x = lax.div(tp, 2)
    base = me - y
    y_right = base + lax.rem(y + 1, 4)
    y_left = base + lax.rem(y + 3, 4)
    up = me + 4
    other = 1 - core
    partner = x * 2 + other
    x_right_i = lax.rem(x + 1, XS)
    x_left_i = lax.rem(x + 3, XS)
    x_far_i = lax.rem(x + 2, XS)
    x_right = x_right_i * 2 + core
    x_left = x_left_i * 2 + core

    def remote(src, dst, send, recv, ctx, tpi):
        return pltpu.make_async_remote_copy(
            src_ref=src, dst_ref=dst, send_sem=send, recv_sem=recv,
            device_id=(ctx, tpi), device_id_type=MESH,
        )

    loads = [
        pltpu.make_async_copy(k_hbm, kv.at[0, 0], local_sem.at[0]),
        pltpu.make_async_copy(v_hbm, kv.at[0, 1], local_sem.at[1]),
        pltpu.make_async_copy(seg_hbm, seg, local_sem.at[2]),
    ]
    for h in range(GROUP):
        loads.append(
            pltpu.make_async_copy(
                q_hbm.at[:, h * HEAD_DIM:(h + 1) * HEAD_DIM],
                q.at[h * TOKENS:(h + 1) * TOKENS, :],
                local_sem.at[3 + h],
            )
        )
    loads.append(pltpu.make_async_copy(rel_hbm, rel, local_sem.at[7]))
    for load in loads:
        load.start()

    barrier = pltpu.get_barrier_semaphore()

    def greet(ctx, tpi):
        pl.semaphore_signal(barrier, inc=1, device_id=(ctx, tpi), device_id_type=MESH)

    greet(me, partner)
    greet(me, x_right)
    greet(me, x_left)
    greet(y_right, tp)
    greet(y_left, tp)

    @pl.when(me < CTX - 4)
    def _():
        greet(me + 4, tp)

    @pl.when(me >= 4)
    def _():
        greet(me - 4, tp)

    @pl.when(me < SLOTS - 1)
    def _():
        for d in range(1, SLOTS):
            @pl.when(me < d)
            def _():
                kv[d] = jnp.zeros((2, TOKENS, HEAD_DIM), BF)

    pl.semaphore_wait(
        barrier, 5 + jnp.where(me < CTX - 4, 1, 0) + jnp.where(me >= 4, 1, 0)
    )

    def kv_copy(number, half, src, dst, ctx):
        return (
            remote(
                kv.at[src, half], kv.at[dst, half], kv_send.at[number, half], kv_recv.at[dst, half], ctx, tp
            ),
            (ctx >= dst) & (ctx < CTX),
        )

    def start(pair):
        copy, exists = pair

        @pl.when(exists)
        def _():
            copy.start()

    def arrive(slot, half):
        @pl.when(me >= slot)
        def _():
            remote(
                kv.at[slot, half], kv.at[slot, half], kv_send.at[0, half], kv_recv.at[slot, half], me, tp
            ).wait_recv()

    right_src = jnp.where(y < 3, 0, 8)
    right_dst = jnp.where(y < 3, 1, 5)
    left_src = jnp.where(y > 0, 8, 0)
    left_dst = jnp.where(y > 0, 7, 3)
    next_right_dst = jnp.where(y < 3, 5, 1)
    next_left_dst = jnp.where(y > 0, 3, 7)
    relay_right_src = jnp.where(y < 3, 1, 5)
    relay_left_src = jnp.where(y > 0, 7, 3)

    def up_one(half):
        return kv_copy(0, half, 0, 4, up)

    def up_two(half):
        return kv_copy(1, half, 4, 8, up)

    def right_zero(half):
        return kv_copy(2, half, right_src, right_dst, y_right)

    def left_zero(half):
        return kv_copy(3, half, left_src, left_dst, y_left)

    def right_one(half):
        return kv_copy(4, half, 4, next_right_dst, y_right)

    def left_one(half):
        return kv_copy(5, half, 4, next_left_dst, y_left)

    def relay_right(half):
        return kv_copy(6, half, relay_right_src, 2, y_right)

    def relay_left(half):
        return kv_copy(7, half, relay_left_src, 6, y_left)

    loads[0].wait()
    start(up_one(0))
    loads[1].wait()
    start(up_one(1))

    @pl.when(y < 3)
    def _():
        start(right_zero(0))
        start(right_zero(1))

    @pl.when(y == 0)
    def _():
        start(left_zero(0))
        start(left_zero(1))

    w_copies = []
    for i in range(XS):
        w_copies.append(
            pltpu.make_async_copy(
                w_hbm.at[:, pl.ds(pl.multiple_of((2 * i + core) * FEAT, FEAT), FEAT)],
                w.at[core, i], w_local_sem.at[i],
            )
        )
        w_copies.append(
            remote(
                w_hbm.at[:, pl.ds(pl.multiple_of((2 * i + other) * FEAT, FEAT), FEAT)],
                w.at[core, i], w_send.at[i], w_recv.at[i], me, partner,
            )
        )
    for copy in w_copies:
        copy.start()

    for load in loads[2:]:
        load.wait()

    own_seg = jnp.broadcast_to(seg[pl.ds(me, 1), :].astype(F32), (TOKENS, TOKENS)).T
    row_at = lax.broadcasted_iota(jnp.int32, (TOKENS, TOKENS), 0)
    key_at = lax.broadcasted_iota(jnp.int32, (TOKENS, TOKENS), 1)

    def score_block(slot, first=False):
        key_seg = seg[pl.ds(lax.rem(me + CTX - slot, CTX), 1), :].astype(F32)
        visible = own_seg == key_seg
        if first:
            visible = visible & (key_at <= row_at)
        for h in range(GROUP):
            rows = pl.ds(h * TOKENS, TOKENS)
            s = dot_nt(q[rows, :], kv[slot, 0])
            s = jnp.where(visible, s, MASKED)
            score[slot, rows, :] = s
            if first:
                peak[rows, :] = s
            else:
                peak[rows, :] = jnp.maximum(peak[rows, :], s)
        values_flipped[slot] = kv[slot, 1].T

    score_block(0, True)

    for half in range(2):
        arrive(4, half)
        start(up_two(half))
        start(right_one(half))
        start(left_one(half))
    score_block(4)

    inner_y = (y == 1) | (y == 2)
    outer_y = (y == 0) | (y == 3)

    @pl.when(y > 0)
    def _():
        for half in range(2):
            arrive(1, half)

            @pl.when(y < 3)
            def _():
                start(relay_right(half))

    @pl.when(y == 3)
    def _():
        for half in range(2):
            arrive(3, half)

    for half in range(2):
        arrive(8, half)

        @pl.when(y > 0)
        def _():
            start(left_zero(half))

        @pl.when(y == 3)
        def _():
            start(right_zero(half))

    score_block(jnp.where(y > 0, 1, 8))

    one_left = jnp.where(y > 0, 5, 1)
    one_right = jnp.where(y < 3, 3, 7)
    for half in range(2):
        arrive(one_left, half)

        @pl.when(outer_y)
        def _():
            start(relay_right(half))

        arrive(one_right, half)

        @pl.when(outer_y)
        def _():
            start(relay_left(half))

    score_block(jnp.where(y > 0, 8, 1))
    score_block(5 - jnp.where(y > 0, 0, 2))
    @pl.when(y == 0)
    def _():
        for half in range(2):
            arrive(5, half)

    @pl.when(y < 3)
    def _():
        for half in range(2):
            arrive(7, half)

            @pl.when(inner_y)
            def _():
                start(relay_left(half))

    score_block(jnp.where(y > 0, 3, 5))
    score_block(7)
    for half in range(2):
        arrive(2, half)
    score_block(2)
    for half in range(2):
        arrive(6, half)
    score_block(6)

    values = kv[:, 1].reshape(SLOTS * TOKENS, HEAD_DIM)
    for h in range(GROUP):
        rows = pl.ds(h * TOKENS, TOKENS)
        top = jnp.max(peak[rows, :], axis=1, keepdims=True)
        top = jnp.broadcast_to(top, (TOKENS, TOKENS))
        total = jnp.zeros((TOKENS, TOKENS), F32)
        for slot in range(SLOTS):
            e = jnp.exp2((score[slot, rows, :] - top) * SCALE2)
            total = total + e
            score[slot, rows, :] = e
            weight[rows, slot * TOKENS:(slot + 1) * TOKENS] = e.astype(BF)
        inv = 1.0 / jnp.broadcast_to(jnp.sum(total, axis=1, keepdims=True), (TOKENS, TOKENS))
        columns = slice(h * HEAD_DIM, (h + 1) * HEAD_DIM)
        inverse[:, columns] = inv
        summed = dot_nn(weight[rows, :], values)
        att[core, :, columns] = (summed * inv).astype(BF)

    a_copy = remote(att.at[core], att.at[core], a_send, a_recv, me, partner)
    a_copy.start()
    for copy in w_copies[0::2]:
        copy.wait()
    for copy in w_copies[1::2]:
        copy.wait_recv()
    remote(att.at[other], att.at[other], a_send, a_recv, me, partner).wait_recv()

    def project(i):
        return dot_nn(att[core], w[core, i]) + dot_nn(att[other], w[other, i])

    quarter = [pl.ds(i * QUARTER, QUARTER) for i in range(4)]

    def rs(kind, i, src, dst, tpi):
        return remote(src, dst, rs_send.at[kind, i], rs_recv.at[kind, i], me, tpi)

    def rs_far(i):
        return rs(0, i, far_out.at[quarter[i]], far_in.at[quarter[i]], x_left if i % 2 else x_right)

    def rs_near(i):
        if i % 2:
            return rs(1, i, right_out.at[quarter[i]], left_in.at[quarter[i]], x_right)
        return rs(1, i, left_out.at[quarter[i]], right_in.at[quarter[i]], x_left)

    def rs_merged(i):
        if i % 2:
            return rs(2, i, left_out.at[quarter[i]], right_in.at[quarter[i]], x_left)
        return rs(2, i, right_out.at[quarter[i]], left_in.at[quarter[i]], x_right)

    far_out[...] = project(x_far_i).astype(BF)
    for i in range(4):
        rs_far(i).start()
    near[0] = project(x_right_i)
    for i in (1, 3):
        right_out[quarter[i], :] = near[0, quarter[i], :].astype(BF)
        rs_near(i).start()
    near[1] = project(x_left_i)
    for i in (0, 2):
        left_out[quarter[i], :] = near[1, quarter[i], :].astype(BF)
        rs_near(i).start()
    near[2] = project(x)
    for i in range(4):
        rs_far(i).wait_recv()
        merged = (near[i % 2, quarter[i], :] + far_in[quarter[i], :].astype(F32)).astype(BF)
        if i % 2:
            left_out[quarter[i], :] = merged
        else:
            right_out[quarter[i], :] = merged
        rs_merged(i).start()

    def ag(kind, i, owner, tpi):
        return remote(
            ratio.at[owner, quarter[i]], ratio.at[owner, quarter[i]],
            ag_send.at[kind, i], ag_recv.at[kind, i], me, tpi,
        )

    def ag_first(i, owner):
        return ag(0, i, owner, x_left if i % 2 else x_right)

    def ag_second(i, owner):
        return ag(1, i, owner, x_right if i % 2 else x_left)

    def ag_relay(i, owner):
        return ag(2, i, owner, x_left if i % 2 else x_right)

    for half in range(2):
        for i in (2 * half, 2 * half + 1):
            rs_near(i).wait_recv()
            rs_merged(i).wait_recv()
            rows = quarter[i]
            total = near[2, rows, :] + left_in[rows, :].astype(F32) + right_in[rows, :].astype(F32)
            ratio[x, rows, :] = (rel[rows, :].astype(F32) * total / (total * total + 1.0)).astype(BF)
            ag_first(i, x).start()
    for i in range(4):
        ag_second(i, x).start()
    back_other = dot_nt(ratio[x], w[other, x])
    back_own = dot_nt(ratio[x], w[core, x])
    for i in range(4):
        owner = x_right_i if i % 2 else x_left_i
        ag_first(i, owner).wait_recv()
        ag_relay(i, owner).start()
    for i in range(4):
        ag_second(i, x_left_i if i % 2 else x_right_i).wait_recv()
    for owner in (x_left_i, x_right_i):
        back_other += dot_nt(ratio[owner], w[other, owner])
        back_own += dot_nt(ratio[owner], w[core, owner])
    for i in range(4):
        ag_relay(i, x_far_i).wait_recv()
    back_other += dot_nt(ratio[x_far_i], w[other, x_far_i])
    cross_out[...] = back_other.astype(BF)
    cross = remote(cross_out, cross_in, c_send, c_recv, me, partner)
    cross.start()
    back_own += dot_nt(ratio[x_far_i], w[core, x_far_i])
    cross.wait_recv()
    a = att[core].astype(F32)
    carried = a * (back_own + cross_in[...].astype(F32))
    heads[...] = carried.astype(BF)
    scaled = carried * a / (a * a + 1.0) * inverse[...]
    for h in range(GROUP):
        passed[h * TOKENS:(h + 1) * TOKENS, :] = scaled[:, h * HEAD_DIM:(h + 1) * HEAD_DIM].astype(BF)

    def term(slot):
        total = jnp.zeros((TOKENS, TOKENS), F32)
        for h in range(GROUP):
            rows = pl.ds(h * TOKENS, TOKENS)
            total = total + score[slot, rows, :] * dot_nn(passed[rows, :], values_flipped[slot])
        return jnp.sum(total, axis=0, keepdims=True)

    def term_copy(slot):
        return remote(
            term_out.at[slot], term_in.at[slot], t_send.at[slot], t_recv.at[slot],
            me - slot, tp,
        )

    for slot in range(SLOTS - 1, 0, -1):
        term_out[slot] = term(slot)

        @pl.when(me >= slot)
        def _():
            term_copy(slot).start()

        @pl.when(me + slot >= CTX)
        def _():
            term_in[slot] = jnp.zeros((1, TOKENS), F32)

    own = term(0)
    for slot in range(1, SLOTS):
        @pl.when(me + slot < CTX)
        def _():
            term_copy(slot).wait_recv()

        own = own + term_in[slot]
    tokens_ref[...] = own

    for copy in w_copies[1::2]:
        copy.wait_send()
    for half in range(2):
        for make in (up_one, up_two, right_zero, left_zero, right_one, left_one, relay_right, relay_left):
            copy, exists = make(half)

            @pl.when(exists)
            def _():
                copy.wait_send()
    a_copy.wait_send()
    for i in range(4):
        owner = x_right_i if i % 2 else x_left_i
        for copy in (
            rs_far(i), rs_near(i), rs_merged(i), ag_first(i, x), ag_second(i, x), ag_relay(i, owner)
        ):
            copy.wait_send()
    cross.wait_send()
    for slot in range(1, SLOTS):
        @pl.when(me >= slot)
        def _():
            term_copy(slot).wait_send()


def leave(heads, tokens, heads_out, tokens_out, sem):
    copies = [
        pltpu.make_async_copy(heads, heads_out, sem.at[0]),
        pltpu.make_async_copy(tokens, tokens_out, sem.at[1]),
    ]
    for copy in copies:
        copy.start()
    for copy in copies:
        copy.wait()


def on_device(queries, keys, values, w_out, relevance_out, segment_ids):
    anywhere = pl.BlockSpec(memory_space=pl.ANY)
    vmem, dma = pltpu.VMEM, pltpu.SemaphoreType.DMA
    heads, tokens = pl.pallas_call(
        kernel,
        out_shape=(
            pltpu.VMEM((TOKENS, GROUP * HEAD_DIM), BF),
            pltpu.VMEM((1, TOKENS), F32),
        ),
        in_specs=[anywhere] * 6,
        out_specs=(pl.BlockSpec(memory_space=pltpu.VMEM), pl.BlockSpec(memory_space=pltpu.VMEM)),
        scratch_shapes=[
            vmem((ROWS, HEAD_DIM), BF),
            vmem((SLOTS, 2, TOKENS, HEAD_DIM), BF),
            vmem((2, XS, FEAT, FEAT), BF),
            vmem((TOKENS, FEAT), BF),
            vmem((CTX, TOKENS), jnp.int32),
            vmem((SLOTS, ROWS, TOKENS), F32),
            vmem((ROWS, SLOTS * TOKENS), BF),
            vmem((ROWS, TOKENS), F32),
            vmem((2, TOKENS, FEAT), BF),
            vmem((TOKENS, FEAT), BF),
            vmem((TOKENS, FEAT), BF),
            vmem((TOKENS, FEAT), BF),
            vmem((TOKENS, FEAT), BF),
            vmem((TOKENS, FEAT), BF),
            vmem((TOKENS, FEAT), BF),
            vmem((3, TOKENS, FEAT), F32),
            vmem((XS, TOKENS, FEAT), BF),
            vmem((TOKENS, FEAT), BF),
            vmem((TOKENS, FEAT), BF),
            vmem((SLOTS, HEAD_DIM, TOKENS), BF),
            vmem((ROWS, HEAD_DIM), BF),
            vmem((TOKENS, FEAT), F32),
            vmem((SLOTS, 1, TOKENS), F32),
            vmem((SLOTS, 1, TOKENS), F32),
            dma((8,)), dma((XS,)), dma((XS,)), dma((XS,)),
            dma((8, 2)), dma((SLOTS, 2)), dma, dma,
            dma((3, 4)), dma((3, 4)), dma((3, 4)), dma((3, 4)), dma, dma,
            dma((SLOTS,)), dma((SLOTS,)),
        ],
        compiler_params=pltpu.CompilerParams(
            collective_id=0, has_side_effects=True, vmem_limit_bytes=60 << 20
        ),
        name="relevance",
    )(queries, keys, values, w_out, relevance_out, segment_ids.reshape(CTX, TOKENS))
    heads, tokens = pl.pallas_call(
        leave,
        out_shape=(
            jax.ShapeDtypeStruct((TOKENS, GROUP * HEAD_DIM), BF),
            jax.ShapeDtypeStruct((1, TOKENS), F32),
        ),
        in_specs=[pl.BlockSpec(memory_space=pltpu.VMEM)] * 2,
        out_specs=(anywhere, anywhere),
        scratch_shapes=[dma((2,))],
        name="leave",
    )(*[pltpu.with_memory_space_constraint(a, pltpu.VMEM) for a in (heads, tokens)])
    return heads, tokens.T


def solution(mesh):
    placed = (P("ctx", "tp"), P("ctx", "tp"), P("ctx", "tp"), P("tp", None), P("ctx", "tp"), P())
    return jax.shard_map(
        on_device,
        mesh=mesh,
        in_specs=placed,
        out_specs=(P("ctx", "tp"), P("ctx", "tp")),
        check_vma=False,
    )
```

```python
import jax
import jax.numpy as jnp
from jax import lax
from jax.experimental import pallas as pl
from jax.experimental.pallas import tpu as pltpu
from jax.sharding import PartitionSpec as P

MESH = pl.DeviceIdType.MESH
HEAD_DIM = 128
GROUP = 4
TOKENS = 128
ROWS = TOKENS * GROUP
SLOTS = 9
CTX = 64
XS = 4
FEAT = 512
QUARTER = TOKENS // 4
BF = jnp.bfloat16
F32 = jnp.float32
MASKED = -1e30
SCALE2 = HEAD_DIM ** (-0.5) * 1.4426950408889634


def dot_nt(a, b):
    return lax.dot_general(a, b, (((1,), (1,)), ((), ())), preferred_element_type=F32)


def dot_nn(a, b):
    return jnp.dot(a, b, preferred_element_type=F32)


def kernel(
    q_hbm, k_hbm, v_hbm, w_hbm, rel_hbm, seg_hbm, heads, tokens_ref,
    q, kv, w, rel, seg, score, weight, peak, att, far_out, far_in, right_out, left_out, left_in, right_in, near,
    ratio, cross_out, cross_in, values_flipped, passed, inverse, term_out, term_in,
    local_sem, w_local_sem, w_send, w_recv, kv_send, kv_recv, a_send, a_recv,
    rs_send, rs_recv, ag_send, ag_recv, c_send, c_recv, t_send, t_recv,
):
    me = lax.axis_index("ctx")
    tp = lax.axis_index("tp")
    y = lax.rem(me, 4)
    core = lax.rem(tp, 2)
    x = lax.div(tp, 2)
    base = me - y
    y_right = base + lax.rem(y + 1, 4)
    y_left = base + lax.rem(y + 3, 4)
    up = me + 4
    other = 1 - core
    partner = x * 2 + other
    x_right_i = lax.rem(x + 1, XS)
    x_left_i = lax.rem(x + 3, XS)
    x_far_i = lax.rem(x + 2, XS)
    x_right = x_right_i * 2 + core
    x_left = x_left_i * 2 + core

    def remote(src, dst, send, recv, ctx, tpi):
        return pltpu.make_async_remote_copy(
            src_ref=src, dst_ref=dst, send_sem=send, recv_sem=recv,
            device_id=(ctx, tpi), device_id_type=MESH,
        )

    loads = [
        pltpu.make_async_copy(k_hbm, kv.at[0, 0], local_sem.at[0]),
        pltpu.make_async_copy(v_hbm, kv.at[0, 1], local_sem.at[1]),
        pltpu.make_async_copy(seg_hbm, seg, local_sem.at[2]),
        pltpu.make_async_copy(rel_hbm, rel, local_sem.at[3]),
    ]
    for h in range(GROUP):
        loads.append(
            pltpu.make_async_copy(
                q_hbm.at[:, h * HEAD_DIM:(h + 1) * HEAD_DIM],
                q.at[h * TOKENS:(h + 1) * TOKENS, :],
                local_sem.at[4],
            )
        )
    for load in loads:
        load.start()

    barrier = pltpu.get_barrier_semaphore()

    def greet(ctx, tpi):
        pl.semaphore_signal(barrier, inc=1, device_id=(ctx, tpi), device_id_type=MESH)

    greet(me, partner)
    greet(me, x_right)
    greet(me, x_left)
    greet(base + lax.rem(y + 2, 4), tp)
    greet(y_right, tp)
    greet(y_left, tp)

    @pl.when(me < CTX - 4)
    def _():
        greet(me + 4, tp)

    @pl.when(me >= 4)
    def _():
        greet(me - 4, tp)

    @pl.when(me < SLOTS - 1)
    def _():
        for d in range(1, SLOTS):
            @pl.when(me < d)
            def _():
                kv[d] = jnp.zeros((2, TOKENS, HEAD_DIM), BF)

    pl.semaphore_wait(
        barrier, 6 + jnp.where(me < CTX - 4, 1, 0) + jnp.where(me >= 4, 1, 0)
    )

    def kv_copy(number, half, src, dst, ctx):
        return (
            remote(
                kv.at[src, half], kv.at[dst, half], kv_send.at[number], kv_recv.at[dst, half], ctx, tp
            ),
            (ctx >= dst) & (ctx < CTX),
        )

    def start(pair):
        copy, exists = pair

        @pl.when(exists)
        def _():
            copy.start()

    def arrive(slot, half):
        @pl.when(me >= slot)
        def _():
            remote(
                kv.at[slot, half], kv.at[slot, half], kv_send.at[0], kv_recv.at[slot, half], me, tp
            ).wait_recv()

    outer_y = (y == 0) | (y == 3)
    right_src = jnp.where(y < 3, 0, 8)
    right_dst = jnp.where(y < 3, 1, 5)
    left_src = jnp.where(y > 0, 8, 0)
    left_dst = jnp.where(y > 0, 7, 3)
    next_right_dst = jnp.where(y < 3, 5, 1)
    next_left_dst = jnp.where(y > 0, 3, 7)
    relay_right_src = jnp.where(y < 3, 1, 5)
    relay_left_src = jnp.where(y > 0, 7, 3)

    def up_one(half):
        return kv_copy(0, half, 0, 4, up)

    def up_two(half):
        return kv_copy(1, half, 4, 8, up)

    def right_zero(half):
        return kv_copy(2, half, right_src, right_dst, y_right)

    def left_zero(half):
        return kv_copy(3, half, left_src, left_dst, y_left)

    def right_one(half):
        return kv_copy(4, half, 4, next_right_dst, y_right)

    def left_one(half):
        return kv_copy(5, half, 4, next_left_dst, y_left)

    def relay_right(half):
        return kv_copy(6, half, relay_right_src, 2, y_right)

    def relay_left(half):
        copy, exists = kv_copy(7, half, relay_left_src, 6, y_left)
        return copy, exists & outer_y

    def far_back(half):
        copy, exists = kv_copy(8, half, 8, 6, me - 2)
        return copy, exists & (y >= 2)

    loads[0].wait()
    start(up_one(0))
    loads[1].wait()
    start(up_one(1))

    @pl.when(y < 3)
    def _():
        start(right_zero(0))
        start(right_zero(1))

    @pl.when(y == 0)
    def _():
        start(left_zero(0))
        start(left_zero(1))

    w_copies = []
    for i in range(XS):
        w_copies.append(
            pltpu.make_async_copy(
                w_hbm.at[:, pl.ds(pl.multiple_of((2 * i + core) * FEAT, FEAT), FEAT)],
                w.at[core, i], w_local_sem,
            )
        )
        w_copies.append(
            remote(
                w_hbm.at[:, pl.ds(pl.multiple_of((2 * i + other) * FEAT, FEAT), FEAT)],
                w.at[core, i], w_send, w_recv, me, partner,
            )
        )
    for copy in w_copies:
        copy.start()

    for load in loads[2:4]:
        load.wait()
    pltpu.make_async_copy(q, q, local_sem.at[4]).wait()

    own_seg = jnp.broadcast_to(seg[pl.ds(me, 1), :].astype(F32), (TOKENS, TOKENS)).T
    row_at = lax.broadcasted_iota(jnp.int32, (TOKENS, TOKENS), 0)
    key_at = lax.broadcasted_iota(jnp.int32, (TOKENS, TOKENS), 1)

    def score_block(slot, first=False):
        key_seg = seg[pl.ds(lax.rem(me + CTX - slot, CTX), 1), :].astype(F32)
        visible = own_seg == key_seg
        if first:
            visible = visible & (key_at <= row_at)
        for h in range(GROUP):
            rows = pl.ds(h * TOKENS, TOKENS)
            s = dot_nt(q[rows, :], kv[slot, 0])
            s = jnp.where(visible, s, MASKED)
            score[slot, rows, :] = s
            if first:
                peak[rows, :] = s
            else:
                peak[rows, :] = jnp.maximum(peak[rows, :], s)
        values_flipped[slot] = kv[slot, 1].T

    score_block(0, True)

    for half in range(2):
        arrive(4, half)
        start(up_two(half))
        start(right_one(half))
        start(left_one(half))
    score_block(4)


    @pl.when(y > 0)
    def _():
        for half in range(2):
            arrive(1, half)

            @pl.when(y < 3)
            def _():
                start(relay_right(half))

    @pl.when(y == 3)
    def _():
        for half in range(2):
            arrive(3, half)

    for half in range(2):
        arrive(8, half)

        @pl.when(y > 0)
        def _():
            start(left_zero(half))

        @pl.when(y == 3)
        def _():
            start(right_zero(half))

        start(far_back(half))

    score_block(jnp.where(y > 0, 1, 8))

    one_left = jnp.where(y > 0, 5, 1)
    one_right = jnp.where(y < 3, 3, 7)
    for half in range(2):
        arrive(one_left, half)

        @pl.when(outer_y)
        def _():
            start(relay_right(half))

        arrive(one_right, half)

        start(relay_left(half))

    score_block(jnp.where(y > 0, 8, 1))
    score_block(5 - jnp.where(y > 0, 0, 2))
    @pl.when(y == 0)
    def _():
        for half in range(2):
            arrive(5, half)

    @pl.when(y < 3)
    def _():
        for half in range(2):
            arrive(7, half)

    score_block(jnp.where(y > 0, 3, 5))
    score_block(7)
    for half in range(2):
        arrive(2, half)
    score_block(2)
    for half in range(2):
        arrive(6, half)
    score_block(6)

    values = kv[:, 1].reshape(SLOTS * TOKENS, HEAD_DIM)
    for h in range(GROUP):
        rows = pl.ds(h * TOKENS, TOKENS)
        top = jnp.max(peak[rows, :], axis=1, keepdims=True)
        top = jnp.broadcast_to(top, (TOKENS, TOKENS))
        total = jnp.zeros((TOKENS, TOKENS), F32)
        for slot in range(SLOTS):
            e = jnp.exp2((score[slot, rows, :] - top) * SCALE2)
            total = total + e
            score[slot, rows, :] = e
            weight[rows, slot * TOKENS:(slot + 1) * TOKENS] = e.astype(BF)
        inv = 1.0 / jnp.broadcast_to(jnp.sum(total, axis=1, keepdims=True), (TOKENS, TOKENS))
        columns = slice(h * HEAD_DIM, (h + 1) * HEAD_DIM)
        inverse[:, columns] = inv
        summed = dot_nn(weight[rows, :], values)
        att[core, :, columns] = (summed * inv).astype(BF)

    a_copy = remote(att.at[core], att.at[core], a_send, a_recv, me, partner)
    a_copy.start()
    pltpu.make_async_copy(w.at[core], w.at[core], w_local_sem).wait()
    remote(w.at[core], w.at[other], w_send, w_recv, me, partner).wait_recv()
    remote(att.at[other], att.at[other], a_send, a_recv, me, partner).wait_recv()

    def project(i):
        return dot_nn(att[core], w[core, i]) + dot_nn(att[other], w[other, i])

    quarter = [pl.ds(i * QUARTER, QUARTER) for i in range(4)]

    def rs(kind, i, src, dst, tpi):
        return remote(src, dst, rs_send, rs_recv.at[4 + i // 2 if kind else i], me, tpi)

    def rs_far(i):
        return rs(0, i, far_out.at[quarter[i]], far_in.at[quarter[i]], x_left if i % 2 else x_right)

    def rs_near(i):
        if i % 2:
            return rs(1, i, right_out.at[quarter[i]], left_in.at[quarter[i]], x_right)
        return rs(1, i, left_out.at[quarter[i]], right_in.at[quarter[i]], x_left)

    def rs_merged(i):
        if i % 2:
            return rs(2, i, left_out.at[quarter[i]], right_in.at[quarter[i]], x_left)
        return rs(2, i, right_out.at[quarter[i]], left_in.at[quarter[i]], x_right)

    far_out[...] = project(x_far_i).astype(BF)
    for i in range(4):
        rs_far(i).start()
    near[0] = project(x_right_i)
    for i in (1, 3):
        right_out[quarter[i], :] = near[0, quarter[i], :].astype(BF)
        rs_near(i).start()
    near[1] = project(x_left_i)
    for i in (0, 2):
        left_out[quarter[i], :] = near[1, quarter[i], :].astype(BF)
        rs_near(i).start()
    near[2] = project(x)
    for i in range(4):
        rs_far(i).wait_recv()
        merged = (near[i % 2, quarter[i], :] + far_in[quarter[i], :].astype(F32)).astype(BF)
        if i % 2:
            left_out[quarter[i], :] = merged
        else:
            right_out[quarter[i], :] = merged
        rs_merged(i).start()

    def ag(kind, i, owner, tpi):
        return remote(
            ratio.at[owner, quarter[i]], ratio.at[owner, quarter[i]],
            ag_send, ag_recv.at[3 + kind if kind else i], me, tpi,
        )

    def ag_first(i, owner):
        return ag(0, i, owner, x_left if i % 2 else x_right)

    def ag_second(i, owner):
        return ag(1, i, owner, x_right if i % 2 else x_left)

    def ag_relay(i, owner):
        return ag(2, i, owner, x_left if i % 2 else x_right)

    for half in range(2):
        remote(left_in, left_in, rs_send, rs_recv.at[4 + half], me, x_left).wait_recv()
        for i in (2 * half, 2 * half + 1):
            rows = quarter[i]
            total = near[2, rows, :] + left_in[rows, :].astype(F32) + right_in[rows, :].astype(F32)
            ratio[x, rows, :] = (rel[rows, :].astype(F32) * total / (total * total + 1.0)).astype(BF)
            ag_first(i, x).start()
    for i in range(4):
        ag_second(i, x).start()
    back_other = dot_nt(ratio[x], w[other, x])
    back_own = dot_nt(ratio[x], w[core, x])
    for i in range(4):
        owner = x_right_i if i % 2 else x_left_i
        ag_first(i, owner).wait_recv()
        ag_relay(i, owner).start()
    remote(ratio.at[x], ratio.at[x_left_i], ag_send, ag_recv.at[4], me, x_left).wait_recv()
    for owner in (x_left_i, x_right_i):
        back_other += dot_nt(ratio[owner], w[other, owner])
        back_own += dot_nt(ratio[owner], w[core, owner])
    remote(ratio.at[x], ratio.at[x_far_i], ag_send, ag_recv.at[5], me, x_left).wait_recv()
    back_other += dot_nt(ratio[x_far_i], w[other, x_far_i])
    cross_out[...] = back_other.astype(BF)
    cross = remote(cross_out, cross_in, c_send, c_recv, me, partner)
    cross.start()
    back_own += dot_nt(ratio[x_far_i], w[core, x_far_i])
    cross.wait_recv()
    a = att[core].astype(F32)
    carried = a * (back_own + cross_in[...].astype(F32))
    heads[...] = carried.astype(BF)
    scaled = carried * a / (a * a + 1.0) * inverse[...]
    for h in range(GROUP):
        passed[h * TOKENS:(h + 1) * TOKENS, :] = scaled[:, h * HEAD_DIM:(h + 1) * HEAD_DIM].astype(BF)

    def term(slot):
        total = jnp.zeros((TOKENS, TOKENS), F32)
        for h in range(GROUP):
            rows = pl.ds(h * TOKENS, TOKENS)
            total = total + score[slot, rows, :] * dot_nn(passed[rows, :], values_flipped[slot])
        return jnp.sum(total, axis=0, keepdims=True)

    def term_copy(slot):
        return remote(
            term_out.at[slot], term_in.at[slot], t_send, t_recv,
            me - slot, tp,
        )

    for slot in range(SLOTS - 1, 0, -1):
        term_out[slot] = term(slot)
    for slot in range(SLOTS - 1, 0, -1):
        @pl.when(me >= slot)
        def _():
            term_copy(slot).start()

        @pl.when(me + slot >= CTX)
        def _():
            term_in[slot] = jnp.zeros((1, TOKENS), F32)

    own = term(0)
    for count in range(1, SLOTS):
        @pl.when(jnp.minimum(SLOTS - 1, CTX - 1 - me) == count)
        def _():
            some = pl.ds(1, count)
            remote(term_out.at[some], term_in.at[some], t_send, t_recv, me, tp).wait_recv()

    for slot in range(1, SLOTS):
        own = own + term_in[slot]
    tokens_ref[...] = own

    remote(w.at[core], w.at[other], w_send, w_recv, me, partner).wait_send()
    for number, make in enumerate(
        (up_one, up_two, right_zero, left_zero, right_one, left_one, relay_right, relay_left, far_back)
    ):
        exists = make(0)[1]

        @pl.when(exists)
        def _():
            remote(kv.at[0], kv.at[0], kv_send.at[number], kv_recv.at[0, 0], me, tp).wait_send()

    a_copy.wait_send()
    twelve = w.at[0, 0, pl.ds(0, 3 * TOKENS)]
    remote(twelve, twelve, rs_send, rs_recv.at[0], me, x_left).wait_send()
    remote(twelve, twelve, ag_send, ag_recv.at[0], me, x_left).wait_send()
    cross.wait_send()
    for count in range(1, SLOTS):
        @pl.when(jnp.minimum(SLOTS - 1, me) == count)
        def _():
            some = pl.ds(1, count)
            remote(term_out.at[some], term_in.at[some], t_send, t_recv, me, tp).wait_send()


def leave(heads, tokens, heads_out, tokens_out, sem):
    copies = [
        pltpu.make_async_copy(heads, heads_out, sem.at[0]),
        pltpu.make_async_copy(tokens, tokens_out, sem.at[1]),
    ]
    for copy in copies:
        copy.start()
    for copy in copies:
        copy.wait()


def on_device(queries, keys, values, w_out, relevance_out, segment_ids):
    anywhere = pl.BlockSpec(memory_space=pl.ANY)
    vmem, dma = pltpu.VMEM, pltpu.SemaphoreType.DMA
    heads, tokens = pl.pallas_call(
        kernel,
        out_shape=(
            pltpu.VMEM((TOKENS, GROUP * HEAD_DIM), BF),
            pltpu.VMEM((1, TOKENS), F32),
        ),
        in_specs=[anywhere] * 6,
        out_specs=(pl.BlockSpec(memory_space=pltpu.VMEM), pl.BlockSpec(memory_space=pltpu.VMEM)),
        scratch_shapes=[
            vmem((ROWS, HEAD_DIM), BF),
            vmem((SLOTS, 2, TOKENS, HEAD_DIM), BF),
            vmem((2, XS, FEAT, FEAT), BF),
            vmem((TOKENS, FEAT), BF),
            vmem((CTX, TOKENS), jnp.int32),
            vmem((SLOTS, ROWS, TOKENS), F32),
            vmem((ROWS, SLOTS * TOKENS), BF),
            vmem((ROWS, TOKENS), F32),
            vmem((2, TOKENS, FEAT), BF),
            vmem((TOKENS, FEAT), BF),
            vmem((TOKENS, FEAT), BF),
            vmem((TOKENS, FEAT), BF),
            vmem((TOKENS, FEAT), BF),
            vmem((TOKENS, FEAT), BF),
            vmem((TOKENS, FEAT), BF),
            vmem((3, TOKENS, FEAT), F32),
            vmem((XS, TOKENS, FEAT), BF),
            vmem((TOKENS, FEAT), BF),
            vmem((TOKENS, FEAT), BF),
            vmem((SLOTS, HEAD_DIM, TOKENS), BF),
            vmem((ROWS, HEAD_DIM), BF),
            vmem((TOKENS, FEAT), F32),
            vmem((SLOTS, 1, TOKENS), F32),
            vmem((SLOTS, 1, TOKENS), F32),
            dma((5,)), dma, dma, dma,
            dma((9,)), dma((SLOTS, 2)), dma, dma,
            dma, dma((6,)), dma, dma((6,)), dma, dma,
            dma, dma,
        ],
        compiler_params=pltpu.CompilerParams(
            collective_id=0, has_side_effects=True, vmem_limit_bytes=60 << 20
        ),
        name="relevance",
    )(queries, keys, values, w_out, relevance_out, segment_ids.reshape(CTX, TOKENS))
    heads, tokens = pl.pallas_call(
        leave,
        out_shape=(
            jax.ShapeDtypeStruct((TOKENS, GROUP * HEAD_DIM), BF),
            jax.ShapeDtypeStruct((1, TOKENS), F32),
        ),
        in_specs=[pl.BlockSpec(memory_space=pltpu.VMEM)] * 2,
        out_specs=(anywhere, anywhere),
        scratch_shapes=[dma((2,))],
        name="leave",
    )(*[pltpu.with_memory_space_constraint(a, pltpu.VMEM) for a in (heads, tokens)])
    return heads, tokens.T


def solution(mesh):
    placed = (P("ctx", "tp"), P("ctx", "tp"), P("ctx", "tp"), P("tp", None), P("ctx", "tp"), P())
    return jax.shard_map(
        on_device,
        mesh=mesh,
        in_specs=placed,
        out_specs=(P("ctx", "tp"), P("ctx", "tp")),
        check_vma=False,
    )
```

```python
import jax
import jax.numpy as jnp
from jax import lax
from jax.experimental import pallas as pl
from jax.experimental.pallas import tpu as pltpu
from jax.sharding import PartitionSpec as P

MESH = pl.DeviceIdType.MESH
HEAD_DIM = 128
GROUP = 4
TOKENS = 128
ROWS = TOKENS * GROUP
SLOTS = 9
CTX = 64
XS = 4
FEAT = 512
QUARTER = TOKENS // 4
BF = jnp.bfloat16
F32 = jnp.float32
MASKED = -1e30
SCALE2 = HEAD_DIM ** (-0.5) * 1.4426950408889634


def dot_nt(a, b):
    return lax.dot_general(a, b, (((1,), (1,)), ((), ())), preferred_element_type=F32)


def dot_nn(a, b):
    return jnp.dot(a, b, preferred_element_type=F32)


def kernel(
    q_hbm, k_hbm, v_hbm, w_hbm, rel_hbm, seg_hbm, heads, tokens_ref,
    q, kv, w, rel, seg, score, weight, peak, att, far_out, far_in, right_out, left_out, left_in, right_in, near,
    ratio, cross_out, cross_in, values_flipped, flipped, back, passed, inverse, term_out, term_in,
    local_sem, w_local_sem, w_send, w_recv, kv_send, kv_recv, a_send, a_recv,
    rs_send, rs_recv, ag_send, ag_recv, c_send, c_recv, t_send, t_recv,
):
    me = lax.axis_index("ctx")
    tp = lax.axis_index("tp")
    y = lax.rem(me, 4)
    core = lax.rem(tp, 2)
    x = lax.div(tp, 2)
    base = me - y
    y_right = base + lax.rem(y + 1, 4)
    y_left = base + lax.rem(y + 3, 4)
    up = me + 4
    other = 1 - core
    partner = x * 2 + other
    x_right_i = lax.rem(x + 1, XS)
    x_left_i = lax.rem(x + 3, XS)
    x_far_i = lax.rem(x + 2, XS)
    x_right = x_right_i * 2 + core
    x_left = x_left_i * 2 + core

    def remote(src, dst, send, recv, ctx, tpi):
        return pltpu.make_async_remote_copy(
            src_ref=src, dst_ref=dst, send_sem=send, recv_sem=recv,
            device_id=(ctx, tpi), device_id_type=MESH,
        )

    loads = [
        pltpu.make_async_copy(k_hbm, kv.at[0, 0], local_sem.at[0]),
        pltpu.make_async_copy(v_hbm, kv.at[0, 1], local_sem.at[1]),
        pltpu.make_async_copy(seg_hbm, seg, local_sem.at[2]),
        pltpu.make_async_copy(rel_hbm, rel, local_sem.at[3]),
    ]
    for h in range(GROUP):
        loads.append(
            pltpu.make_async_copy(
                q_hbm.at[:, h * HEAD_DIM:(h + 1) * HEAD_DIM],
                q.at[h * TOKENS:(h + 1) * TOKENS, :],
                local_sem.at[4],
            )
        )
    for load in loads:
        load.start()

    barrier = pltpu.get_barrier_semaphore()

    def greet(ctx, tpi):
        pl.semaphore_signal(barrier, inc=1, device_id=(ctx, tpi), device_id_type=MESH)

    greet(me, partner)
    greet(me, x_right)
    greet(me, x_left)
    greet(base + lax.rem(y + 2, 4), tp)
    greet(y_right, tp)
    greet(y_left, tp)

    @pl.when(me < CTX - 4)
    def _():
        greet(me + 4, tp)

    @pl.when(me >= 4)
    def _():
        greet(me - 4, tp)

    @pl.when(me < SLOTS - 1)
    def _():
        for d in range(1, SLOTS):
            @pl.when(me < d)
            def _():
                kv[d] = jnp.zeros((2, TOKENS, HEAD_DIM), BF)

    pl.semaphore_wait(
        barrier, 6 + jnp.where(me < CTX - 4, 1, 0) + jnp.where(me >= 4, 1, 0)
    )

    def kv_copy(number, half, src, dst, ctx):
        return (
            remote(
                kv.at[src, half], kv.at[dst, half], kv_send.at[number], kv_recv.at[dst, half], ctx, tp
            ),
            (ctx >= dst) & (ctx < CTX),
        )

    def start(pair):
        copy, exists = pair

        @pl.when(exists)
        def _():
            copy.start()

    def arrive(slot, half):
        @pl.when(me >= slot)
        def _():
            remote(
                kv.at[slot, half], kv.at[slot, half], kv_send.at[0], kv_recv.at[slot, half], me, tp
            ).wait_recv()

    right_src = jnp.where(y < 3, 0, 8)
    right_dst = jnp.where(y < 3, 1, 5)
    left_src = jnp.where(y > 0, 8, 0)
    left_dst = jnp.where(y > 0, 7, 3)
    next_right_dst = jnp.where(y < 3, 5, 1)
    next_left_dst = jnp.where(y > 0, 3, 7)
    relay_right_src = jnp.where(y < 3, 1, 5)

    def up_one(half):
        return kv_copy(0, half, 0, 4, up)

    def up_two(half):
        return kv_copy(1, half, 4, 8, up)

    def right_zero(half):
        return kv_copy(2, half, right_src, right_dst, y_right)

    def left_zero(half):
        return kv_copy(3, half, left_src, left_dst, y_left)

    def right_one(half):
        return kv_copy(4, half, 4, next_right_dst, y_right)

    def left_one(half):
        return kv_copy(5, half, 4, next_left_dst, y_left)

    def relay_right(half):
        copy, exists = kv_copy(6, half, relay_right_src, 2, y_right)
        return copy, exists & ((y == 1) | (y == 2))

    def below_two(half):
        return kv_copy(7, half, 4, jnp.where(y < 2, 6, 2), jnp.where(y < 2, me + 2, me - 2))

    def far_back(half):
        copy, exists = kv_copy(8, half, 8, 6, me - 2)
        return copy, exists & (y >= 2)

    loads[0].wait()
    start(up_one(0))
    loads[1].wait()
    start(up_one(1))

    @pl.when(y < 3)
    def _():
        start(right_zero(0))
        start(right_zero(1))

    @pl.when(y == 0)
    def _():
        start(left_zero(0))
        start(left_zero(1))

    w_copies = []
    for i in range(XS):
        w_copies.append(
            pltpu.make_async_copy(
                w_hbm.at[:, pl.ds(pl.multiple_of((2 * i + core) * FEAT, FEAT), FEAT)],
                w.at[core, i], w_local_sem,
            )
        )
        w_copies.append(
            remote(
                w_hbm.at[:, pl.ds(pl.multiple_of((2 * i + other) * FEAT, FEAT), FEAT)],
                w.at[core, i], w_send, w_recv, me, partner,
            )
        )
    for copy in w_copies:
        copy.start()

    for load in loads[2:4]:
        load.wait()
    pltpu.make_async_copy(q, q, local_sem.at[4]).wait()

    own_seg = jnp.broadcast_to(seg[pl.ds(me, 1), :].astype(F32), (TOKENS, TOKENS)).T
    row_at = lax.broadcasted_iota(jnp.int32, (TOKENS, TOKENS), 0)
    key_at = lax.broadcasted_iota(jnp.int32, (TOKENS, TOKENS), 1)

    def score_block(slot, first=False):
        key_seg = seg[pl.ds(lax.rem(me + CTX - slot, CTX), 1), :].astype(F32)
        visible = own_seg == key_seg
        if first:
            visible = visible & (key_at <= row_at)
        for h in range(GROUP):
            rows = pl.ds(h * TOKENS, TOKENS)
            s = dot_nt(q[rows, :], kv[slot, 0])
            s = jnp.where(visible, s, MASKED)
            score[slot, rows, :] = s
            if first:
                peak[rows, :] = s
            else:
                peak[rows, :] = jnp.maximum(peak[rows, :], s)

    score_block(0, True)

    for half in range(2):
        arrive(4, half)
        start(up_two(half))
        start(below_two(half))
        start(right_one(half))
        start(left_one(half))
    score_block(4)


    @pl.when(y > 0)
    def _():
        for half in range(2):
            arrive(1, half)

            @pl.when(y < 3)
            def _():
                start(relay_right(half))

    @pl.when(y == 3)
    def _():
        for half in range(2):
            arrive(3, half)

    for half in range(2):
        arrive(8, half)

        @pl.when(y > 0)
        def _():
            start(left_zero(half))

        @pl.when(y == 3)
        def _():
            start(right_zero(half))

        start(far_back(half))

    score_block(jnp.where(y > 0, 1, 8))

    one_left = jnp.where(y > 0, 5, 1)
    one_right = jnp.where(y < 3, 3, 7)
    for half in range(2):
        arrive(one_left, half)
        arrive(one_right, half)

    score_block(jnp.where(y > 0, 8, 1))
    score_block(5 - jnp.where(y > 0, 0, 2))
    @pl.when(y == 0)
    def _():
        for half in range(2):
            arrive(5, half)

    @pl.when(y < 3)
    def _():
        for half in range(2):
            arrive(7, half)

    score_block(jnp.where(y > 0, 3, 5))
    score_block(7)
    for half in range(2):
        arrive(2, half)
    score_block(2)
    for half in range(2):
        arrive(6, half)
    score_block(6)

    values = kv[:, 1].reshape(SLOTS * TOKENS, HEAD_DIM)
    for h in range(GROUP):
        rows = pl.ds(h * TOKENS, TOKENS)
        top = jnp.max(peak[rows, :], axis=1, keepdims=True)
        top = jnp.broadcast_to(top, (TOKENS, TOKENS))
        total = jnp.zeros((TOKENS, TOKENS), F32)
        for slot in range(SLOTS):
            e = jnp.exp2((score[slot, rows, :] - top) * SCALE2)
            total = total + e
            score[slot, rows, :] = e
            weight[rows, slot * TOKENS:(slot + 1) * TOKENS] = e.astype(BF)
        inv = 1.0 / jnp.broadcast_to(jnp.sum(total, axis=1, keepdims=True), (TOKENS, TOKENS))
        columns = slice(h * HEAD_DIM, (h + 1) * HEAD_DIM)
        inverse[:, columns] = inv
        summed = dot_nn(weight[rows, :], values)
        att[core, :, columns] = (summed * inv).astype(BF)

    a_copy = remote(att.at[core], att.at[core], a_send, a_recv, me, partner)
    a_copy.start()
    pltpu.make_async_copy(w.at[core], w.at[core], w_local_sem).wait()
    remote(w.at[core], w.at[other], w_send, w_recv, me, partner).wait_recv()
    remote(att.at[other], att.at[other], a_send, a_recv, me, partner).wait_recv()

    def project(i):
        return dot_nn(att[core], w[core, i]) + dot_nn(att[other], w[other, i])

    quarter = [pl.ds(i * QUARTER, QUARTER) for i in range(4)]

    def rs(kind, i, src, dst, tpi):
        return remote(src, dst, rs_send, rs_recv.at[4 + i // 2 if kind else i], me, tpi)

    def rs_far(i):
        return rs(0, i, far_out.at[quarter[i]], far_in.at[quarter[i]], x_left if i % 2 else x_right)

    def rs_near(i):
        if i % 2:
            return rs(1, i, right_out.at[quarter[i]], left_in.at[quarter[i]], x_right)
        return rs(1, i, left_out.at[quarter[i]], right_in.at[quarter[i]], x_left)

    def rs_merged(i):
        if i % 2:
            return rs(2, i, left_out.at[quarter[i]], right_in.at[quarter[i]], x_left)
        return rs(2, i, right_out.at[quarter[i]], left_in.at[quarter[i]], x_right)

    far_out[...] = project(x_far_i).astype(BF)
    for i in range(4):
        rs_far(i).start()
    near[0] = project(x_right_i)
    near[1] = project(x_left_i)
    near[2] = project(x)
    for i in range(4):
        if i % 2:
            right_out[quarter[i], :] = near[0, quarter[i], :].astype(BF)
        else:
            left_out[quarter[i], :] = near[1, quarter[i], :].astype(BF)
    for i in range(4):
        rs_near(i).start()
    for slot in range(SLOTS):
        values_flipped[slot] = kv[slot, 1].T
    for j in range(2):
        flipped[j] = w[j, x_far_i].T
    for i in range(4):
        rs_far(i).wait_recv()
        merged = (near[i % 2, quarter[i], :] + far_in[quarter[i], :].astype(F32)).astype(BF)
        if i % 2:
            left_out[quarter[i], :] = merged
        else:
            right_out[quarter[i], :] = merged
        rs_merged(i).start()

    def ag(kind, i, owner, tpi):
        return remote(
            ratio.at[owner, quarter[i]], ratio.at[owner, quarter[i]],
            ag_send, ag_recv.at[3 + kind if kind else i], me, tpi,
        )

    def ag_first(i, owner):
        return ag(0, i, owner, x_left if i % 2 else x_right)

    def ag_second(i, owner):
        return ag(1, i, owner, x_right if i % 2 else x_left)

    def ag_relay(i, owner):
        return ag(2, i, owner, x_left if i % 2 else x_right)

    for half in range(2):
        remote(left_in, left_in, rs_send, rs_recv.at[4 + half], me, x_left).wait_recv()
        for i in (2 * half, 2 * half + 1):
            rows = quarter[i]
            total = near[2, rows, :] + left_in[rows, :].astype(F32) + right_in[rows, :].astype(F32)
            ratio[x, rows, :] = (rel[rows, :].astype(F32) * total / (total * total + 1.0)).astype(BF)
            ag_first(i, x).start()
    back[0] = dot_nt(ratio[x], w[other, x])
    back[1] = dot_nt(ratio[x], w[core, x])
    for i in range(4):
        ag_second(i, x).start()
    for i in range(4):
        owner = x_right_i if i % 2 else x_left_i
        ag_first(i, owner).wait_recv()
        ag_relay(i, owner).start()
    remote(ratio.at[x], ratio.at[x_left_i], ag_send, ag_recv.at[4], me, x_left).wait_recv()
    for owner in (x_left_i, x_right_i):
        back[0] += dot_nt(ratio[owner], w[other, owner])
        back[1] += dot_nt(ratio[owner], w[core, owner])
    remote(ratio.at[x], ratio.at[x_far_i], ag_send, ag_recv.at[5], me, x_left).wait_recv()
    back_other = back[0] + dot_nn(ratio[x_far_i], flipped[other])
    cross_out[...] = back_other.astype(BF)
    cross = remote(cross_out, cross_in, c_send, c_recv, me, partner)
    cross.start()
    back_own = back[1] + dot_nn(ratio[x_far_i], flipped[core])
    cross.wait_recv()
    a = att[core].astype(F32)
    carried = a * (back_own + cross_in[...].astype(F32))
    heads[...] = carried.astype(BF)
    scaled = carried * a / (a * a + 1.0) * inverse[...]
    for h in range(GROUP):
        passed[h * TOKENS:(h + 1) * TOKENS, :] = scaled[:, h * HEAD_DIM:(h + 1) * HEAD_DIM].astype(BF)

    def term(slot):
        total = jnp.zeros((TOKENS, TOKENS), F32)
        for h in range(GROUP):
            rows = pl.ds(h * TOKENS, TOKENS)
            total = total + score[slot, rows, :] * dot_nn(passed[rows, :], values_flipped[slot])
        return jnp.sum(total, axis=0, keepdims=True)

    def term_copy(slot):
        return remote(
            term_out.at[slot], term_in.at[slot], t_send, t_recv,
            me - slot, tp,
        )

    for slot in range(SLOTS - 1, 0, -1):
        term_out[slot] = term(slot)
    for slot in range(SLOTS - 1, 0, -1):
        @pl.when(me >= slot)
        def _():
            term_copy(slot).start()

        @pl.when(me + slot >= CTX)
        def _():
            term_in[slot] = jnp.zeros((1, TOKENS), F32)

    own = term(0)
    for count in range(1, SLOTS):
        @pl.when(jnp.minimum(SLOTS - 1, CTX - 1 - me) == count)
        def _():
            some = pl.ds(1, count)
            remote(term_out.at[some], term_in.at[some], t_send, t_recv, me, tp).wait_recv()

    for slot in range(1, SLOTS):
        own = own + term_in[slot]
    tokens_ref[...] = own

    remote(w.at[core], w.at[other], w_send, w_recv, me, partner).wait_send()
    for number, make in enumerate(
        (up_one, up_two, right_zero, left_zero, right_one, left_one, relay_right, below_two, far_back)
    ):
        exists = make(0)[1]

        @pl.when(exists)
        def _():
            remote(kv.at[0], kv.at[0], kv_send.at[number], kv_recv.at[0, 0], me, tp).wait_send()

    a_copy.wait_send()
    twelve = w.at[0, 0, pl.ds(0, 3 * TOKENS)]
    remote(twelve, twelve, rs_send, rs_recv.at[0], me, x_left).wait_send()
    remote(twelve, twelve, ag_send, ag_recv.at[0], me, x_left).wait_send()
    cross.wait_send()
    for count in range(1, SLOTS):
        @pl.when(jnp.minimum(SLOTS - 1, me) == count)
        def _():
            some = pl.ds(1, count)
            remote(term_out.at[some], term_in.at[some], t_send, t_recv, me, tp).wait_send()


def leave(heads, tokens, heads_out, tokens_out, sem):
    copies = [
        pltpu.make_async_copy(heads, heads_out, sem.at[0]),
        pltpu.make_async_copy(tokens, tokens_out, sem.at[1]),
    ]
    for copy in copies:
        copy.start()
    for copy in copies:
        copy.wait()


def on_device(queries, keys, values, w_out, relevance_out, segment_ids):
    anywhere = pl.BlockSpec(memory_space=pl.ANY)
    vmem, dma = pltpu.VMEM, pltpu.SemaphoreType.DMA
    heads, tokens = pl.pallas_call(
        kernel,
        out_shape=(
            pltpu.VMEM((TOKENS, GROUP * HEAD_DIM), BF),
            pltpu.VMEM((1, TOKENS), F32),
        ),
        in_specs=[anywhere] * 6,
        out_specs=(pl.BlockSpec(memory_space=pltpu.VMEM), pl.BlockSpec(memory_space=pltpu.VMEM)),
        scratch_shapes=[
            vmem((ROWS, HEAD_DIM), BF),
            vmem((SLOTS, 2, TOKENS, HEAD_DIM), BF),
            vmem((2, XS, FEAT, FEAT), BF),
            vmem((TOKENS, FEAT), BF),
            vmem((CTX, TOKENS), jnp.int32),
            vmem((SLOTS, ROWS, TOKENS), F32),
            vmem((ROWS, SLOTS * TOKENS), BF),
            vmem((ROWS, TOKENS), F32),
            vmem((2, TOKENS, FEAT), BF),
            vmem((TOKENS, FEAT), BF),
            vmem((TOKENS, FEAT), BF),
            vmem((TOKENS, FEAT), BF),
            vmem((TOKENS, FEAT), BF),
            vmem((TOKENS, FEAT), BF),
            vmem((TOKENS, FEAT), BF),
            vmem((3, TOKENS, FEAT), F32),
            vmem((XS, TOKENS, FEAT), BF),
            vmem((TOKENS, FEAT), BF),
            vmem((TOKENS, FEAT), BF),
            vmem((SLOTS, HEAD_DIM, TOKENS), BF),
            vmem((2, FEAT, FEAT), BF),
            vmem((2, TOKENS, FEAT), F32),
            vmem((ROWS, HEAD_DIM), BF),
            vmem((TOKENS, FEAT), F32),
            vmem((SLOTS, 1, TOKENS), F32),
            vmem((SLOTS, 1, TOKENS), F32),
            dma((5,)), dma, dma, dma,
            dma((9,)), dma((SLOTS, 2)), dma, dma,
            dma, dma((6,)), dma, dma((6,)), dma, dma,
            dma, dma,
        ],
        compiler_params=pltpu.CompilerParams(
            collective_id=0, has_side_effects=True, vmem_limit_bytes=60 << 20
        ),
        name="relevance",
    )(queries, keys, values, w_out, relevance_out, segment_ids.reshape(CTX, TOKENS))
    heads, tokens = pl.pallas_call(
        leave,
        out_shape=(
            jax.ShapeDtypeStruct((TOKENS, GROUP * HEAD_DIM), BF),
            jax.ShapeDtypeStruct((1, TOKENS), F32),
        ),
        in_specs=[pl.BlockSpec(memory_space=pltpu.VMEM)] * 2,
        out_specs=(anywhere, anywhere),
        scratch_shapes=[dma((2,))],
        name="leave",
    )(*[pltpu.with_memory_space_constraint(a, pltpu.VMEM) for a in (heads, tokens)])
    return heads, tokens.T


def solution(mesh):
    placed = (P("ctx", "tp"), P("ctx", "tp"), P("ctx", "tp"), P("tp", None), P("ctx", "tp"), P())
    return jax.shard_map(
        on_device,
        mesh=mesh,
        in_specs=placed,
        out_specs=(P("ctx", "tp"), P("ctx", "tp")),
        check_vma=False,
    )
```

```python
import jax
import jax.numpy as jnp
from jax import lax
from jax.experimental import pallas as pl
from jax.experimental.pallas import tpu as pltpu
from jax.sharding import PartitionSpec as P

MESH = pl.DeviceIdType.MESH
HEAD_DIM = 128
GROUP = 4
TOKENS = 128
ROWS = TOKENS * GROUP
SLOTS = 9
CTX = 64
XS = 4
FEAT = 512
QUARTER = TOKENS // 4
BF = jnp.bfloat16
F32 = jnp.float32
MASKED = -1e30
SCALE2 = HEAD_DIM ** (-0.5) * 1.4426950408889634


def dot_nt(a, b):
    return lax.dot_general(a, b, (((1,), (1,)), ((), ())), preferred_element_type=F32)


def dot_nn(a, b):
    return jnp.dot(a, b, preferred_element_type=F32)


def kernel(
    q_hbm, k_hbm, v_hbm, w_hbm, rel_hbm, seg_hbm, heads, tokens_ref,
    q, kv, w, rel, seg, score, weight, peak, att, far_out, far_in, right_out, left_out, left_in, right_in, near,
    ratio, cross_out, cross_in, values_flipped, flipped, back, passed, inverse, term_out, term_in,
    local_sem, w_local_sem, sent, w_recv, kv_send, kv_recv, a_recv,
    rs_recv, ag_recv, c_recv, t_send, t_recv,
):
    me = lax.axis_index("ctx")
    tp = lax.axis_index("tp")
    y = lax.rem(me, 4)
    core = lax.rem(tp, 2)
    x = lax.div(tp, 2)
    base = me - y
    y_right = base + lax.rem(y + 1, 4)
    y_left = base + lax.rem(y + 3, 4)
    up = me + 4
    other = 1 - core
    partner = x * 2 + other
    x_right_i = lax.rem(x + 1, XS)
    x_left_i = lax.rem(x + 3, XS)
    x_far_i = lax.rem(x + 2, XS)
    x_right = x_right_i * 2 + core
    x_left = x_left_i * 2 + core

    def remote(src, dst, send, recv, ctx, tpi):
        return pltpu.make_async_remote_copy(
            src_ref=src, dst_ref=dst, send_sem=send, recv_sem=recv,
            device_id=(ctx, tpi), device_id_type=MESH,
        )

    loads = [
        pltpu.make_async_copy(k_hbm, kv.at[0, 0], local_sem.at[0]),
        pltpu.make_async_copy(v_hbm, kv.at[0, 1], local_sem.at[1]),
        pltpu.make_async_copy(seg_hbm, seg, local_sem.at[2]),
        pltpu.make_async_copy(rel_hbm, rel, local_sem.at[2]),
    ]
    for h in range(GROUP):
        loads.append(
            pltpu.make_async_copy(
                q_hbm.at[:, h * HEAD_DIM:(h + 1) * HEAD_DIM],
                q.at[h * TOKENS:(h + 1) * TOKENS, :],
                local_sem.at[2],
            )
        )
    for load in loads:
        load.start()

    barrier = pltpu.get_barrier_semaphore()

    def greet(ctx, tpi):
        pl.semaphore_signal(barrier, inc=1, device_id=(ctx, tpi), device_id_type=MESH)

    greet(me, partner)
    greet(me, x_right)
    greet(me, x_left)
    greet(base + lax.rem(y + 2, 4), tp)
    greet(y_right, tp)
    greet(y_left, tp)

    @pl.when(me < CTX - 4)
    def _():
        greet(me + 4, tp)

    @pl.when(me >= 4)
    def _():
        greet(me - 4, tp)

    @pl.when(me < SLOTS - 1)
    def _():
        for d in range(1, SLOTS):
            @pl.when(me < d)
            def _():
                kv[d] = jnp.zeros((2, TOKENS, HEAD_DIM), BF)

    pl.semaphore_wait(
        barrier, 6 + jnp.where(me < CTX - 4, 1, 0) + jnp.where(me >= 4, 1, 0)
    )

    def kv_copy(number, half, src, dst, ctx):
        return (
            remote(
                kv.at[src, half], kv.at[dst, half], kv_send, kv_recv.at[dst, half], ctx, tp
            ),
            (ctx >= dst) & (ctx < CTX),
        )

    def start(pair):
        copy, exists = pair

        @pl.when(exists)
        def _():
            copy.start()

    def arrive(slot, half):
        @pl.when(me >= slot)
        def _():
            remote(
                kv.at[slot, half], kv.at[slot, half], kv_send, kv_recv.at[slot, half], me, tp
            ).wait_recv()

    right_src = jnp.where(y < 3, 0, 8)
    right_dst = jnp.where(y < 3, 1, 5)
    left_src = jnp.where(y > 0, 8, 0)
    left_dst = jnp.where(y > 0, 7, 3)
    next_right_dst = jnp.where(y < 3, 5, 1)
    next_left_dst = jnp.where(y > 0, 3, 7)
    relay_right_src = jnp.where(y < 3, 1, 5)

    def up_one(half):
        return kv_copy(0, half, 0, 4, up)

    def up_two(half):
        return kv_copy(1, half, 4, 8, up)

    def right_zero(half):
        return kv_copy(2, half, right_src, right_dst, y_right)

    def left_zero(half):
        return kv_copy(3, half, left_src, left_dst, y_left)

    def right_one(half):
        return kv_copy(4, half, 4, next_right_dst, y_right)

    def left_one(half):
        return kv_copy(5, half, 4, next_left_dst, y_left)

    def relay_right(half):
        copy, exists = kv_copy(6, half, relay_right_src, 2, y_right)
        return copy, exists & ((y == 1) | (y == 2))

    def below_two(half):
        return kv_copy(7, half, 4, jnp.where(y < 2, 6, 2), jnp.where(y < 2, me + 2, me - 2))

    def far_back(half):
        copy, exists = kv_copy(8, half, 8, 6, me - 2)
        return copy, exists & (y >= 2)

    loads[0].wait()
    start(up_one(0))
    loads[1].wait()
    start(up_one(1))

    @pl.when(y < 3)
    def _():
        start(right_zero(0))
        start(right_zero(1))

    @pl.when(y == 0)
    def _():
        start(left_zero(0))
        start(left_zero(1))

    w_copies = []
    for i in range(XS):
        w_copies.append(
            pltpu.make_async_copy(
                w_hbm.at[:, pl.ds(pl.multiple_of((2 * i + core) * FEAT, FEAT), FEAT)],
                w.at[core, i], w_local_sem,
            )
        )
        w_copies.append(
            remote(
                w_hbm.at[:, pl.ds(pl.multiple_of((2 * i + other) * FEAT, FEAT), FEAT)],
                w.at[core, i], sent, w_recv, me, partner,
            )
        )
    for copy in w_copies:
        copy.start()

    three = w.at[0, 0, pl.ds(0, 288)]
    pltpu.make_async_copy(three, three, local_sem.at[2]).wait()

    own_seg = jnp.broadcast_to(seg[pl.ds(me, 1), :].astype(F32), (TOKENS, TOKENS)).T
    row_at = lax.broadcasted_iota(jnp.int32, (TOKENS, TOKENS), 0)
    key_at = lax.broadcasted_iota(jnp.int32, (TOKENS, TOKENS), 1)

    def score_block(slot, first=False):
        key_seg = seg[pl.ds(lax.rem(me + CTX - slot, CTX), 1), :].astype(F32)
        visible = own_seg == key_seg
        if first:
            visible = visible & (key_at <= row_at)
        for h in range(GROUP):
            rows = pl.ds(h * TOKENS, TOKENS)
            s = dot_nt(q[rows, :], kv[slot, 0])
            s = jnp.where(visible, s, MASKED)
            score[slot, rows, :] = s
            if first:
                peak[rows, :] = s
            else:
                peak[rows, :] = jnp.maximum(peak[rows, :], s)

    score_block(0, True)

    for half in range(2):
        arrive(4, half)
        start(up_two(half))
        start(below_two(half))
        start(right_one(half))
        start(left_one(half))
    score_block(4)


    @pl.when((y == 1) | (y == 2))
    def _():
        for half in range(2):
            arrive(1, half)
            start(relay_right(half))

    for half in range(2):
        arrive(8, half)

        @pl.when(y > 0)
        def _():
            start(left_zero(half))

        @pl.when(y == 3)
        def _():
            start(right_zero(half))

        start(far_back(half))

    score_block(8)
    orders = ((3, 7, 2, 6, 1, 5), (1, 5, 3, 7, 2, 6), (1, 2, 5, 6, 3, 7), (1, 3, 2, 6, 7, 5))
    for i in range(6):
        by_y = [order[i] for order in orders]
        slot = jnp.where(y == 0, by_y[0], jnp.where(y == 1, by_y[1], jnp.where(y == 2, by_y[2], by_y[3])))
        if i == 0:
            @pl.when((y == 0) | (y == 3))
            def _():
                for half in range(2):
                    arrive(slot, half)
        else:
            for half in range(2):
                arrive(slot, half)
        score_block(slot)

    values = kv[:, 1].reshape(SLOTS * TOKENS, HEAD_DIM)
    for h in range(GROUP):
        rows = pl.ds(h * TOKENS, TOKENS)
        top = jnp.max(peak[rows, :], axis=1, keepdims=True)
        top = jnp.broadcast_to(top, (TOKENS, TOKENS))
        total = jnp.zeros((TOKENS, TOKENS), F32)
        for slot in range(SLOTS):
            e = jnp.exp2((score[slot, rows, :] - top) * SCALE2)
            total = total + e
            score[slot, rows, :] = e
            weight[rows, slot * TOKENS:(slot + 1) * TOKENS] = e.astype(BF)
        inv = 1.0 / jnp.broadcast_to(jnp.sum(total, axis=1, keepdims=True), (TOKENS, TOKENS))
        columns = slice(h * HEAD_DIM, (h + 1) * HEAD_DIM)
        inverse[:, columns] = inv
        summed = dot_nn(weight[rows, :], values)
        att[core, :, columns] = (summed * inv).astype(BF)

    a_copy = remote(att.at[core], att.at[core], sent, a_recv, me, partner)
    a_copy.start()
    pltpu.make_async_copy(w.at[core], w.at[core], w_local_sem).wait()
    remote(w.at[core], w.at[other], sent, w_recv, me, partner).wait_recv()
    remote(att.at[other], att.at[other], sent, a_recv, me, partner).wait_recv()

    def project(i):
        return dot_nn(att[core], w[core, i]) + dot_nn(att[other], w[other, i])

    quarter = [pl.ds(i * QUARTER, QUARTER) for i in range(4)]

    def rs(kind, i, src, dst, tpi):
        return remote(src, dst, sent, rs_recv.at[4 + i // 2 if kind else i], me, tpi)

    def rs_far(i):
        return rs(0, i, far_out.at[quarter[i]], far_in.at[quarter[i]], x_left if i % 2 else x_right)

    def rs_near(i):
        if i % 2:
            return rs(1, i, right_out.at[quarter[i]], left_in.at[quarter[i]], x_right)
        return rs(1, i, left_out.at[quarter[i]], right_in.at[quarter[i]], x_left)

    def rs_merged(i):
        if i % 2:
            return rs(2, i, left_out.at[quarter[i]], right_in.at[quarter[i]], x_left)
        return rs(2, i, right_out.at[quarter[i]], left_in.at[quarter[i]], x_right)

    far_out[...] = project(x_far_i).astype(BF)
    for i in range(4):
        rs_far(i).start()
    near[0] = project(x_right_i)
    near[1] = project(x_left_i)
    near[2] = project(x)
    for i in range(4):
        if i % 2:
            right_out[quarter[i], :] = near[0, quarter[i], :].astype(BF)
        else:
            left_out[quarter[i], :] = near[1, quarter[i], :].astype(BF)
    for i in range(4):
        rs_near(i).start()
    for slot in range(SLOTS):
        values_flipped[slot] = kv[slot, 1].T
    for j in range(2):
        flipped[j] = w[j, x_far_i].T
    for i in range(4):
        rs_far(i).wait_recv()
        merged = (near[i % 2, quarter[i], :] + far_in[quarter[i], :].astype(F32)).astype(BF)
        if i % 2:
            left_out[quarter[i], :] = merged
        else:
            right_out[quarter[i], :] = merged
        rs_merged(i).start()

    def ag(kind, i, owner, tpi):
        return remote(
            ratio.at[owner, quarter[i]], ratio.at[owner, quarter[i]],
            sent, ag_recv.at[3 + kind if kind else i], me, tpi,
        )

    def ag_first(i, owner):
        return ag(0, i, owner, x_left if i % 2 else x_right)

    def ag_second(i, owner):
        return ag(1, i, owner, x_right if i % 2 else x_left)

    def ag_relay(i, owner):
        return ag(2, i, owner, x_left if i % 2 else x_right)

    for half in range(2):
        remote(left_in, left_in, sent, rs_recv.at[4 + half], me, x_left).wait_recv()
        for i in (2 * half, 2 * half + 1):
            rows = quarter[i]
            total = near[2, rows, :] + left_in[rows, :].astype(F32) + right_in[rows, :].astype(F32)
            ratio[x, rows, :] = (rel[rows, :].astype(F32) * total / (total * total + 1.0)).astype(BF)
            ag_first(i, x).start()
    back[0] = dot_nt(ratio[x], w[other, x])
    back[1] = dot_nt(ratio[x], w[core, x])
    for i in range(4):
        ag_second(i, x).start()
    for i in range(4):
        owner = x_right_i if i % 2 else x_left_i
        ag_first(i, owner).wait_recv()
        ag_relay(i, owner).start()
    remote(ratio.at[x], ratio.at[x_left_i], sent, ag_recv.at[4], me, x_left).wait_recv()
    for owner in (x_left_i, x_right_i):
        back[0] += dot_nt(ratio[owner], w[other, owner])
        back[1] += dot_nt(ratio[owner], w[core, owner])
    remote(ratio.at[x], ratio.at[x_far_i], sent, ag_recv.at[5], me, x_left).wait_recv()
    back_other = back[0] + dot_nn(ratio[x_far_i], flipped[other])
    cross_out[...] = back_other.astype(BF)
    cross = remote(cross_out, cross_in, sent, c_recv, me, partner)
    cross.start()
    back_own = back[1] + dot_nn(ratio[x_far_i], flipped[core])
    cross.wait_recv()
    a = att[core].astype(F32)
    carried = a * (back_own + cross_in[...].astype(F32))
    heads[...] = carried.astype(BF)
    scaled = carried * a / (a * a + 1.0) * inverse[...]
    for h in range(GROUP):
        passed[h * TOKENS:(h + 1) * TOKENS, :] = scaled[:, h * HEAD_DIM:(h + 1) * HEAD_DIM].astype(BF)

    def term(slot):
        total = jnp.zeros((TOKENS, TOKENS), F32)
        for h in range(GROUP):
            rows = pl.ds(h * TOKENS, TOKENS)
            total = total + score[slot, rows, :] * dot_nn(passed[rows, :], values_flipped[slot])
        return jnp.sum(total, axis=0, keepdims=True)

    def term_copy(slot):
        return remote(
            term_out.at[slot], term_in.at[slot], t_send, t_recv,
            me - slot, tp,
        )

    for batch in ((8, 7, 6, 5), (4, 3, 2, 1)):
        for slot in batch:
            term_out[slot] = term(slot)
        for slot in batch:
            @pl.when(me >= slot)
            def _():
                term_copy(slot).start()

    for slot in range(1, SLOTS):
        @pl.when(me + slot >= CTX)
        def _():
            term_in[slot] = jnp.zeros((1, TOKENS), F32)

    own = term(0)
    for count in range(1, SLOTS):
        @pl.when(jnp.minimum(SLOTS - 1, CTX - 1 - me) == count)
        def _():
            some = pl.ds(1, count)
            remote(term_out.at[some], term_in.at[some], t_send, t_recv, me, tp).wait_recv()

    for slot in range(1, SLOTS):
        own = own + term_in[slot]
    tokens_ref[...] = own

    copies = 0
    for make in (
        up_one, up_two, right_zero, left_zero, right_one, left_one, relay_right, below_two, far_back
    ):
        copies = copies + jnp.where(make(0)[1], 1, 0)
    for count in range(1, SLOTS + 1):
        @pl.when(copies == count)
        def _():
            some = kv.at[pl.ds(0, count)]
            remote(some, some, kv_send, kv_recv.at[0, 0], me, tp).wait_send()

    everything = w.at[:, 0:3]
    remote(everything, everything, sent, w_recv, me, partner).wait_send()
    for count in range(1, SLOTS):
        @pl.when(jnp.minimum(SLOTS - 1, me) == count)
        def _():
            some = pl.ds(1, count)
            remote(term_out.at[some], term_in.at[some], t_send, t_recv, me, tp).wait_send()


def leave(heads, tokens, heads_out, tokens_out, sem):
    copies = [
        pltpu.make_async_copy(heads, heads_out, sem.at[0]),
        pltpu.make_async_copy(tokens, tokens_out, sem.at[1]),
    ]
    for copy in copies:
        copy.start()
    for copy in copies:
        copy.wait()


def on_device(queries, keys, values, w_out, relevance_out, segment_ids):
    anywhere = pl.BlockSpec(memory_space=pl.ANY)
    vmem, dma = pltpu.VMEM, pltpu.SemaphoreType.DMA
    heads, tokens = pl.pallas_call(
        kernel,
        out_shape=(
            pltpu.VMEM((TOKENS, GROUP * HEAD_DIM), BF),
            pltpu.VMEM((1, TOKENS), F32),
        ),
        in_specs=[anywhere] * 6,
        out_specs=(pl.BlockSpec(memory_space=pltpu.VMEM), pl.BlockSpec(memory_space=pltpu.VMEM)),
        scratch_shapes=[
            vmem((ROWS, HEAD_DIM), BF),
            vmem((SLOTS, 2, TOKENS, HEAD_DIM), BF),
            vmem((2, XS, FEAT, FEAT), BF),
            vmem((TOKENS, FEAT), BF),
            vmem((CTX, TOKENS), jnp.int32),
            vmem((SLOTS, ROWS, TOKENS), F32),
            vmem((ROWS, SLOTS * TOKENS), BF),
            vmem((ROWS, TOKENS), F32),
            vmem((2, TOKENS, FEAT), BF),
            vmem((TOKENS, FEAT), BF),
            vmem((TOKENS, FEAT), BF),
            vmem((TOKENS, FEAT), BF),
            vmem((TOKENS, FEAT), BF),
            vmem((TOKENS, FEAT), BF),
            vmem((TOKENS, FEAT), BF),
            vmem((3, TOKENS, FEAT), F32),
            vmem((XS, TOKENS, FEAT), BF),
            vmem((TOKENS, FEAT), BF),
            vmem((TOKENS, FEAT), BF),
            vmem((SLOTS, HEAD_DIM, TOKENS), BF),
            vmem((2, FEAT, FEAT), BF),
            vmem((2, TOKENS, FEAT), F32),
            vmem((ROWS, HEAD_DIM), BF),
            vmem((TOKENS, FEAT), F32),
            vmem((SLOTS, 1, TOKENS), F32),
            vmem((SLOTS, 1, TOKENS), F32),
            dma((3,)), dma, dma, dma, dma, dma((SLOTS, 2)), dma,
            dma((6,)), dma((6,)), dma, dma, dma,
        ],
        compiler_params=pltpu.CompilerParams(
            collective_id=0, has_side_effects=True, vmem_limit_bytes=60 << 20
        ),
        name="relevance",
    )(queries, keys, values, w_out, relevance_out, segment_ids.reshape(CTX, TOKENS))
    heads, tokens = pl.pallas_call(
        leave,
        out_shape=(
            jax.ShapeDtypeStruct((TOKENS, GROUP * HEAD_DIM), BF),
            jax.ShapeDtypeStruct((1, TOKENS), F32),
        ),
        in_specs=[pl.BlockSpec(memory_space=pltpu.VMEM)] * 2,
        out_specs=(anywhere, anywhere),
        scratch_shapes=[dma((2,))],
        name="leave",
    )(*[pltpu.with_memory_space_constraint(a, pltpu.VMEM) for a in (heads, tokens)])
    return heads, tokens.T


def solution(mesh):
    placed = (P("ctx", "tp"), P("ctx", "tp"), P("ctx", "tp"), P("tp", None), P("ctx", "tp"), P())
    return jax.shard_map(
        on_device,
        mesh=mesh,
        in_specs=placed,
        out_specs=(P("ctx", "tp"), P("ctx", "tp")),
        check_vma=False,
    )
```

```python
import jax
import jax.numpy as jnp
from jax import lax
from jax.experimental import pallas as pl
from jax.experimental.pallas import tpu as pltpu
from jax.sharding import PartitionSpec as P

MESH = pl.DeviceIdType.MESH
HEAD_DIM = 128
GROUP = 4
TOKENS = 128
ROWS = TOKENS * GROUP
SLOTS = 9
CTX = 64
XS = 4
FEAT = 512
QUARTER = TOKENS // 4
BF = jnp.bfloat16
F32 = jnp.float32
MASKED = -1e30
SCALE2 = HEAD_DIM ** (-0.5) * 1.4426950408889634


def dot_nt(a, b):
    return lax.dot_general(a, b, (((1,), (1,)), ((), ())), preferred_element_type=F32)


def dot_nn(a, b):
    return jnp.dot(a, b, preferred_element_type=F32)


def kernel(
    q_hbm, k_hbm, v_hbm, w_hbm, rel_hbm, seg_hbm, heads, tokens_ref,
    q, kv, w, rel, seg, score, weight, peak, att, far_out, far_in, right_out, left_out, left_in, right_in, near,
    ratio, cross_out, cross_in, values_flipped, flipped, back, passed, inverse, term_out, term_in,
    local_sem, w_local_sem, sent, w_recv, kv_send, kv_recv, a_recv,
    rs_recv, ag_recv, c_recv, t_send, t_recv,
):
    me = lax.axis_index("ctx")
    tp = lax.axis_index("tp")
    y = lax.rem(me, 4)
    core = lax.rem(tp, 2)
    x = lax.div(tp, 2)
    base = me - y
    y_right = base + lax.rem(y + 1, 4)
    y_left = base + lax.rem(y + 3, 4)
    up = me + 4
    other = 1 - core
    partner = x * 2 + other
    x_right_i = lax.rem(x + 1, XS)
    x_left_i = lax.rem(x + 3, XS)
    x_far_i = lax.rem(x + 2, XS)
    x_right = x_right_i * 2 + core
    x_left = x_left_i * 2 + core

    def remote(src, dst, send, recv, ctx, tpi):
        return pltpu.make_async_remote_copy(
            src_ref=src, dst_ref=dst, send_sem=send, recv_sem=recv,
            device_id=(ctx, tpi), device_id_type=MESH,
        )

    loads = [
        pltpu.make_async_copy(k_hbm, kv.at[0, 0], local_sem.at[0]),
        pltpu.make_async_copy(v_hbm, kv.at[0, 1], local_sem.at[1]),
        pltpu.make_async_copy(seg_hbm, seg, local_sem.at[2]),
        pltpu.make_async_copy(rel_hbm, rel, local_sem.at[2]),
    ]
    for h in range(GROUP):
        loads.append(
            pltpu.make_async_copy(
                q_hbm.at[:, h * HEAD_DIM:(h + 1) * HEAD_DIM],
                q.at[h * TOKENS:(h + 1) * TOKENS, :],
                local_sem.at[2],
            )
        )
    for load in loads:
        load.start()

    barrier = pltpu.get_barrier_semaphore()

    def greet(ctx, tpi):
        pl.semaphore_signal(barrier, inc=1, device_id=(ctx, tpi), device_id_type=MESH)

    greet(me, partner)
    greet(me, x_right)
    greet(me, x_left)
    greet(base + lax.rem(y + 2, 4), tp)
    greet(y_right, tp)
    greet(y_left, tp)

    @pl.when(me >= 4)
    def _():
        greet(me - 4, tp)

    @pl.when(me < SLOTS - 1)
    def _():
        for d in range(1, SLOTS):
            @pl.when(me < d)
            def _():
                kv[d] = jnp.zeros((2, TOKENS, HEAD_DIM), BF)

    pl.semaphore_wait(
        barrier, 6 + jnp.where(me < CTX - 4, 1, 0)
    )

    def kv_copy(number, half, src, dst, ctx):
        return (
            remote(
                kv.at[src, half], kv.at[dst, half], kv_send, kv_recv.at[dst, half], ctx, tp
            ),
            (ctx >= dst) & (ctx < CTX),
        )

    def start(pair):
        copy, exists = pair

        @pl.when(exists)
        def _():
            copy.start()

    def arrive(slot, half):
        @pl.when(me >= slot)
        def _():
            remote(
                kv.at[slot, half], kv.at[slot, half], kv_send, kv_recv.at[slot, half], me, tp
            ).wait_recv()

    right_src = jnp.where(y < 3, 0, 8)
    right_dst = jnp.where(y < 3, 1, 5)
    left_src = jnp.where(y > 0, 8, 0)
    left_dst = jnp.where(y > 0, 7, 3)
    next_right_dst = jnp.where(y < 3, 5, 1)
    next_left_dst = jnp.where(y > 0, 3, 7)
    relay_right_src = jnp.where(y < 3, 1, 5)

    def up_one(half):
        return kv_copy(0, half, 0, 4, up)

    def up_two(half):
        return kv_copy(1, half, 4, 8, up)

    def right_zero(half):
        return kv_copy(2, half, right_src, right_dst, y_right)

    def left_zero(half):
        return kv_copy(3, half, left_src, left_dst, y_left)

    def right_one(half):
        return kv_copy(4, half, 4, next_right_dst, y_right)

    def left_one(half):
        return kv_copy(5, half, 4, next_left_dst, y_left)

    def relay_right(half):
        copy, exists = kv_copy(6, half, relay_right_src, 2, y_right)
        return copy, exists & ((y == 1) | (y == 2))

    def below_two(half):
        return kv_copy(7, half, 4, jnp.where(y < 2, 6, 2), jnp.where(y < 2, me + 2, me - 2))

    def far_back(half):
        copy, exists = kv_copy(8, half, 8, 6, me - 2)
        return copy, exists & (y >= 2)

    loads[0].wait()
    start(up_one(0))
    loads[1].wait()
    start(up_one(1))

    @pl.when(y < 3)
    def _():
        start(right_zero(0))
        start(right_zero(1))

    @pl.when(y == 0)
    def _():
        start(left_zero(0))
        start(left_zero(1))

    w_copies = []
    for i in range(XS):
        w_copies.append(
            pltpu.make_async_copy(
                w_hbm.at[:, pl.ds(pl.multiple_of((2 * i + core) * FEAT, FEAT), FEAT)],
                w.at[core, i], w_local_sem,
            )
        )
        w_copies.append(
            remote(
                w_hbm.at[:, pl.ds(pl.multiple_of((2 * i + other) * FEAT, FEAT), FEAT)],
                w.at[core, i], sent, w_recv, me, partner,
            )
        )
    for copy in w_copies:
        copy.start()

    three = w.at[0, 0, pl.ds(0, 288)]
    pltpu.make_async_copy(three, three, local_sem.at[2]).wait()

    own_seg = jnp.broadcast_to(seg[pl.ds(me, 1), :].astype(F32), (TOKENS, TOKENS)).T
    row_at = lax.broadcasted_iota(jnp.int32, (TOKENS, TOKENS), 0)
    key_at = lax.broadcasted_iota(jnp.int32, (TOKENS, TOKENS), 1)

    def score_block(slot, first=False):
        key_seg = seg[pl.ds(lax.rem(me + CTX - slot, CTX), 1), :].astype(F32)
        visible = own_seg == key_seg
        if first:
            visible = visible & (key_at <= row_at)
        for h in range(GROUP):
            rows = pl.ds(h * TOKENS, TOKENS)
            s = dot_nt(q[rows, :], kv[slot, 0])
            s = jnp.where(visible, s, MASKED)
            score[slot, rows, :] = s
            if first:
                peak[rows, :] = s
            else:
                peak[rows, :] = jnp.maximum(peak[rows, :], s)

    score_block(0, True)

    for half in range(2):
        arrive(4, half)
        start(up_two(half))
        start(below_two(half))
        start(right_one(half))
        start(left_one(half))
    score_block(4)


    @pl.when((y == 1) | (y == 2))
    def _():
        for half in range(2):
            arrive(1, half)
            start(relay_right(half))

    for half in range(2):
        arrive(8, half)

        @pl.when(y > 0)
        def _():
            start(left_zero(half))

        @pl.when(y == 3)
        def _():
            start(right_zero(half))

        start(far_back(half))

    score_block(8)
    orders = ((3, 7, 2, 6, 1, 5), (1, 5, 3, 7, 2, 6), (1, 2, 5, 6, 3, 7), (1, 3, 2, 6, 7, 5))
    for i in range(6):
        by_y = [order[i] for order in orders]
        slot = jnp.where(y == 0, by_y[0], jnp.where(y == 1, by_y[1], jnp.where(y == 2, by_y[2], by_y[3])))
        if i == 0:
            @pl.when((y == 0) | (y == 3))
            def _():
                for half in range(2):
                    arrive(slot, half)
        else:
            for half in range(2):
                arrive(slot, half)
        score_block(slot)

    values = kv[:, 1].reshape(SLOTS * TOKENS, HEAD_DIM)
    for h in range(GROUP):
        rows = pl.ds(h * TOKENS, TOKENS)
        top = jnp.max(peak[rows, :], axis=1, keepdims=True)
        top = jnp.broadcast_to(top, (TOKENS, TOKENS))
        total = jnp.zeros((TOKENS, TOKENS), F32)
        for slot in range(SLOTS):
            e = jnp.exp2((score[slot, rows, :] - top) * SCALE2)
            total = total + e
            score[slot, rows, :] = e
            weight[rows, slot * TOKENS:(slot + 1) * TOKENS] = e.astype(BF)
        inv = 1.0 / jnp.broadcast_to(jnp.sum(total, axis=1, keepdims=True), (TOKENS, TOKENS))
        columns = slice(h * HEAD_DIM, (h + 1) * HEAD_DIM)
        inverse[:, columns] = inv
        summed = dot_nn(weight[rows, :], values)
        att[core, :, columns] = (summed * inv).astype(BF)

    a_copy = remote(att.at[core], att.at[core], sent, a_recv, me, partner)
    a_copy.start()
    pltpu.make_async_copy(w.at[core], w.at[core], w_local_sem).wait()
    remote(w.at[core], w.at[other], sent, w_recv, me, partner).wait_recv()
    remote(att.at[other], att.at[other], sent, a_recv, me, partner).wait_recv()

    def project(i):
        return dot_nn(att[core], w[core, i]) + dot_nn(att[other], w[other, i])

    quarter = [pl.ds(i * QUARTER, QUARTER) for i in range(4)]

    def rs(kind, i, src, dst, tpi):
        return remote(src, dst, sent, rs_recv.at[4 + i // 2 if kind else i], me, tpi)

    def rs_far(i):
        return rs(0, i, far_out.at[quarter[i]], far_in.at[quarter[i]], x_left if i % 2 else x_right)

    def rs_near(i):
        if i % 2:
            return rs(1, i, right_out.at[quarter[i]], left_in.at[quarter[i]], x_right)
        return rs(1, i, left_out.at[quarter[i]], right_in.at[quarter[i]], x_left)

    def rs_merged(i):
        if i % 2:
            return rs(2, i, left_out.at[quarter[i]], right_in.at[quarter[i]], x_left)
        return rs(2, i, right_out.at[quarter[i]], left_in.at[quarter[i]], x_right)

    far_out[...] = project(x_far_i).astype(BF)
    for i in range(4):
        rs_far(i).start()
    near[0] = project(x_right_i)
    near[1] = project(x_left_i)
    near[2] = project(x)
    for i in range(4):
        if i % 2:
            right_out[quarter[i], :] = near[0, quarter[i], :].astype(BF)
        else:
            left_out[quarter[i], :] = near[1, quarter[i], :].astype(BF)
    for i in range(4):
        rs_near(i).start()
    for slot in range(SLOTS):
        values_flipped[slot] = kv[slot, 1].T
    for j in range(2):
        flipped[j] = w[j, x_far_i].T
    for i in range(4):
        rs_far(i).wait_recv()
        merged = (near[i % 2, quarter[i], :] + far_in[quarter[i], :].astype(F32)).astype(BF)
        if i % 2:
            left_out[quarter[i], :] = merged
        else:
            right_out[quarter[i], :] = merged
        rs_merged(i).start()

    def ag(kind, i, owner, tpi):
        return remote(
            ratio.at[owner, quarter[i]], ratio.at[owner, quarter[i]],
            sent, ag_recv.at[3 + kind if kind else i], me, tpi,
        )

    def ag_first(i, owner):
        return ag(0, i, owner, x_left if i % 2 else x_right)

    def ag_second(i, owner):
        return ag(1, i, owner, x_right if i % 2 else x_left)

    def ag_relay(i, owner):
        return ag(2, i, owner, x_left if i % 2 else x_right)

    for half in range(2):
        remote(left_in, left_in, sent, rs_recv.at[4 + half], me, x_left).wait_recv()
        for i in (2 * half, 2 * half + 1):
            rows = quarter[i]
            total = near[2, rows, :] + left_in[rows, :].astype(F32) + right_in[rows, :].astype(F32)
            ratio[x, rows, :] = (rel[rows, :].astype(F32) * total / (total * total + 1.0)).astype(BF)
            ag_first(i, x).start()
    back[0] = dot_nt(ratio[x], w[other, x])
    back[1] = dot_nt(ratio[x], w[core, x])
    for i in range(4):
        ag_second(i, x).start()
    for i in range(4):
        owner = x_right_i if i % 2 else x_left_i
        ag_first(i, owner).wait_recv()
        ag_relay(i, owner).start()
    remote(ratio.at[x], ratio.at[x_left_i], sent, ag_recv.at[4], me, x_left).wait_recv()
    for owner in (x_left_i, x_right_i):
        back[0] += dot_nt(ratio[owner], w[other, owner])
        back[1] += dot_nt(ratio[owner], w[core, owner])
    remote(ratio.at[x], ratio.at[x_far_i], sent, ag_recv.at[5], me, x_left).wait_recv()
    back_other = back[0] + dot_nn(ratio[x_far_i], flipped[other])
    cross_out[...] = back_other.astype(BF)
    cross = remote(cross_out, cross_in, sent, c_recv, me, partner)
    cross.start()
    back_own = back[1] + dot_nn(ratio[x_far_i], flipped[core])
    cross.wait_recv()
    a = att[core].astype(F32)
    carried = a * (back_own + cross_in[...].astype(F32))
    heads[...] = carried.astype(BF)
    scaled = carried * a / (a * a + 1.0) * inverse[...]
    for h in range(GROUP):
        passed[h * TOKENS:(h + 1) * TOKENS, :] = scaled[:, h * HEAD_DIM:(h + 1) * HEAD_DIM].astype(BF)

    def term(slot):
        total = jnp.zeros((TOKENS, TOKENS), F32)
        for h in range(GROUP):
            rows = pl.ds(h * TOKENS, TOKENS)
            total = total + score[slot, rows, :] * dot_nn(passed[rows, :], values_flipped[slot])
        return jnp.sum(total, axis=0, keepdims=True)

    def term_copy(slot):
        return remote(
            term_out.at[slot], term_in.at[slot], t_send, t_recv,
            me - slot, tp,
        )

    for batch in ((8, 7, 6, 5), (4, 3, 2, 1)):
        for slot in batch:
            term_out[slot] = term(slot)
        for slot in batch:
            @pl.when(me >= slot)
            def _():
                term_copy(slot).start()

    for slot in range(1, SLOTS):
        @pl.when(me + slot >= CTX)
        def _():
            term_in[slot] = jnp.zeros((1, TOKENS), F32)

    own = term(0)
    for count in range(1, SLOTS):
        @pl.when(jnp.minimum(SLOTS - 1, CTX - 1 - me) == count)
        def _():
            some = pl.ds(1, count)
            remote(term_out.at[some], term_in.at[some], t_send, t_recv, me, tp).wait_recv()

    for slot in range(1, SLOTS):
        own = own + term_in[slot]
    tokens_ref[...] = own

    copies = 0
    for make in (
        up_one, up_two, right_zero, left_zero, right_one, left_one, relay_right, below_two, far_back
    ):
        copies = copies + jnp.where(make(0)[1], 1, 0)
    for count in range(1, SLOTS + 1):
        @pl.when(copies == count)
        def _():
            some = kv.at[pl.ds(0, count)]
            remote(some, some, kv_send, kv_recv.at[0, 0], me, tp).wait_send()

    everything = w.at[:, 0:3]
    remote(everything, everything, sent, w_recv, me, partner).wait_send()
    for count in range(1, SLOTS):
        @pl.when(jnp.minimum(SLOTS - 1, me) == count)
        def _():
            some = pl.ds(1, count)
            remote(term_out.at[some], term_in.at[some], t_send, t_recv, me, tp).wait_send()


def leave(heads, tokens, heads_out, tokens_out, sem):
    copies = [
        pltpu.make_async_copy(heads, heads_out, sem.at[0]),
        pltpu.make_async_copy(tokens, tokens_out, sem.at[1]),
    ]
    for copy in copies:
        copy.start()
    for copy in copies:
        copy.wait()


def on_device(queries, keys, values, w_out, relevance_out, segment_ids):
    anywhere = pl.BlockSpec(memory_space=pl.ANY)
    vmem, dma = pltpu.VMEM, pltpu.SemaphoreType.DMA
    heads, tokens = pl.pallas_call(
        kernel,
        out_shape=(
            pltpu.VMEM((TOKENS, GROUP * HEAD_DIM), BF),
            pltpu.VMEM((1, TOKENS), F32),
        ),
        in_specs=[anywhere] * 6,
        out_specs=(pl.BlockSpec(memory_space=pltpu.VMEM), pl.BlockSpec(memory_space=pltpu.VMEM)),
        scratch_shapes=[
            vmem((ROWS, HEAD_DIM), BF),
            vmem((SLOTS, 2, TOKENS, HEAD_DIM), BF),
            vmem((2, XS, FEAT, FEAT), BF),
            vmem((TOKENS, FEAT), BF),
            vmem((CTX, TOKENS), jnp.int32),
            vmem((SLOTS, ROWS, TOKENS), F32),
            vmem((ROWS, SLOTS * TOKENS), BF),
            vmem((ROWS, TOKENS), F32),
            vmem((2, TOKENS, FEAT), BF),
            vmem((TOKENS, FEAT), BF),
            vmem((TOKENS, FEAT), BF),
            vmem((TOKENS, FEAT), BF),
            vmem((TOKENS, FEAT), BF),
            vmem((TOKENS, FEAT), BF),
            vmem((TOKENS, FEAT), BF),
            vmem((3, TOKENS, FEAT), F32),
            vmem((XS, TOKENS, FEAT), BF),
            vmem((TOKENS, FEAT), BF),
            vmem((TOKENS, FEAT), BF),
            vmem((SLOTS, HEAD_DIM, TOKENS), BF),
            vmem((2, FEAT, FEAT), BF),
            vmem((2, TOKENS, FEAT), F32),
            vmem((ROWS, HEAD_DIM), BF),
            vmem((TOKENS, FEAT), F32),
            vmem((SLOTS, 1, TOKENS), F32),
            vmem((SLOTS, 1, TOKENS), F32),
            dma((3,)), dma, dma, dma, dma, dma((SLOTS, 2)), dma,
            dma((6,)), dma((6,)), dma, dma, dma,
        ],
        compiler_params=pltpu.CompilerParams(
            collective_id=0, has_side_effects=True, vmem_limit_bytes=60 << 20
        ),
        name="relevance",
    )(queries, keys, values, w_out, relevance_out, segment_ids.reshape(CTX, TOKENS))
    heads, tokens = pl.pallas_call(
        leave,
        out_shape=(
            jax.ShapeDtypeStruct((TOKENS, GROUP * HEAD_DIM), BF),
            jax.ShapeDtypeStruct((1, TOKENS), F32),
        ),
        in_specs=[pl.BlockSpec(memory_space=pltpu.VMEM)] * 2,
        out_specs=(anywhere, anywhere),
        scratch_shapes=[dma((2,))],
        name="leave",
    )(*[pltpu.with_memory_space_constraint(a, pltpu.VMEM) for a in (heads, tokens)])
    return heads, tokens.T


def solution(mesh):
    placed = (P("ctx", "tp"), P("ctx", "tp"), P("ctx", "tp"), P("tp", None), P("ctx", "tp"), P())
    return jax.shard_map(
        on_device,
        mesh=mesh,
        in_specs=placed,
        out_specs=(P("ctx", "tp"), P("ctx", "tp")),
        check_vma=False,
    )
```
